128 devices in a mesh: track: 8 (over z, core), cross: 16 (over y, x).
Axes of the slice: x: 4, y: 4, z: 4, core: 2. Of those that a mesh axis runs over, the one named last changes fastest.
Arguments:
- direction: float32 [3, 128, 1024, 256], P(None, 'track', 'cross'), may hold values from -6 to 6
- wind: float32 [3, 128, 1024, 256], P(None, 'track', 'cross'), may hold values from -5 to 5
- wind_gradient: float32 [9, 128, 1024, 256], P(None, 'track', 'cross'), may hold values from -3 to 3
- viscosity: float32 [128, 1024, 256], P('track', 'cross'), may hold values from 0.1 to 0.5
- sample_owner: int32 [8, 16, 8192, 1], P('track', 'cross'), may hold values from 0 to 127; in each aligned block of 8192 rows (0 to 8191, 8192 to 16383, ..., all dimensions but the last counted through in order) at most 128 rows name the same one
- sample_cell: int32 [8, 16, 8192], P('track', 'cross'), may hold values from 0 to 262143
- sample_gate: int32 [8, 16, 8192], P('track', 'cross'), may hold values from 0 to 1023
- sight: float32 [3, 128, 1024], P(None, ('track', 'cross')), may hold values from -1.5 to 1.5
- gate_counts: int32 [128, 8], P(('track', 'cross')), may hold values from 1 to 128, 768 in all within a row
- precision: float32 [128, 128, 128], P(('track', 'cross')), as said below
Outputs:
- hessian_product: float32 [3, 128, 1024, 256], P(None, 'track', 'cross')
- weighted_obs: float32 [128, 1024], P(('track', 'cross'))
The draws below stay inside these ranges and needn't reach their ends.
Inputs may be any that keep to these rules, and one draw needn't show every extreme that they name: `sample_owner`: among the 8192 samples of one device no lidar is named more than 128 times, a bound that some block reaches. `gate_counts`: each lidar's counts sum to 768, and the largest is 128. `precision`: each matrix is symmetric with a diagonal that exceeds its row's other entries in sum of magnitudes.
All inputs are finite; a program needn't handle non-finite values.
Results may differ from the reference program's by a relative error of at most 0.0003.
Values sent between devices are 32-bit elements; how exact they have to be, the bound alone decides.
No kernel may reach another device: no remote copies, remote signals or barrier semaphores. Data moves between devices by JAX's collectives and lax.ppermute only.
A program may use at most 384 MiB of HBM per device.

```python
import math
import jax
import jax.numpy as jnp
import numpy as np
from jax import lax

CX = 16
CY = 64
NZ = 256
S_DEV = 8192
BEAMS = 8
GATES = 128
OWNERS = 128
CAP = 128
OBS_DEV = 1024
NX = 128
NY = 1024
N_TRACK = 8
N_CROSS = 16


def draw_precision(key, part):
    first, second = jax.random.split(jax.random.fold_in(key, 17))
    diagonal = 1.0 + jax.random.uniform(first, (OWNERS, GATES), jnp.float32)
    spread = 1.2 / GATES
    offdiag = jax.random.uniform(second, (OWNERS, GATES, GATES), jnp.float32, -spread, spread)
    offdiag = (offdiag + jnp.swapaxes(offdiag, 1, 2)) * 0.5
    identity = jnp.eye(GATES, dtype=jnp.float32)[None, :, :]
    return offdiag * (1.0 - identity) + identity * diagonal[:, :, None]


def place_ends(drawn, rng, smallest, top_value):
    place = [jax.random.randint(jax.random.fold_in(rng, axis), (), 0, length) for axis, length in enumerate(drawn.shape)]
    longest = drawn.shape.index(max(drawn.shape))
    beside = place[:longest] + [(place[longest] + 1) % drawn.shape[longest]] + place[longest + 1:]
    return drawn.at[tuple(place)].set(smallest).at[tuple(beside)].set(top_value)


def levels(rng, dims, cuts, least, high):
    gain, own = 1.0, jax.random.fold_in(rng, 6)
    for axis_at, parts in cuts:
        draws = jnp.exp(jax.random.uniform(jax.random.fold_in(own, axis_at), (parts,), jnp.float32, least / len(cuts), high / len(cuts)))
        gain = gain * jnp.repeat(draws, dims[axis_at] // parts).reshape([-1 if axis == axis_at else 1 for axis in range(len(dims))])
    return gain


def profile(number_of, total, bound, slope):
    portions = [(1 << 20) // math.isqrt(rank ** slope) + 1 for rank in range(2, number_of + 1)]
    spare, counts = total - bound - (number_of - 1), [1] * (number_of - 1)
    while spare > 0:
        free = [i for i in range(number_of - 1) if counts[i] < bound]
        mass, budget = sum([portions[i] for i in free]), spare
        for i in free:
            more = min(bound - counts[i], max(1, budget * portions[i] // mass), spare)
            counts[i] = counts[i] + more
            spare = spare - more
    return np.array([bound] + counts)


def uneven(stream_key, count, total, limit, slope):
    if count == 2:
        one = jax.random.randint(stream_key, (), max(1, total - limit), min(limit, total - 1) + 1)
        return jnp.stack([one, total - one])
    sizes = jnp.asarray(profile(count, total, limit, slope), jnp.int32)
    twos = (count - 1) // 2
    giver, receiver = sizes[1:1 + 2 * twos:2], sizes[2:2 + 2 * twos:2]
    slack = jnp.minimum(giver - 1, limit - receiver)
    passed = jax.random.randint(jax.random.fold_in(stream_key, 1), (twos,), 0, 1 << 20) % (slack + 1)
    sizes = sizes.at[1:1 + 2 * twos:2].set(giver - passed).at[2:2 + 2 * twos:2].set(receiver + passed)
    return sizes[jax.random.permutation(jax.random.fold_in(stream_key, 2), count)]


def deal_out(stream_key, own, number, rows, number_of, top, bound, skew):
    order = jax.random.permutation(stream_key, number_of)
    heavy_load, common = load_shares(number_of, rows * top, bound, skew, True), load_shares(number_of, rows * top, bound, skew, False)
    places = jnp.arange(number_of)

    def named(lengths, rotation):
        used = int((lengths > 0).sum())
        fixed = max(1, used // 4)
        moved = fixed + (places - fixed + rotation * (used - fixed)) % max(1, number_of - fixed)
        return jnp.zeros((number_of,), jnp.int32).at[order[jnp.where(places < fixed, places, moved)]].set(jnp.asarray(lengths, jnp.int32))

    lengths = jnp.where(number % 4 == 0, named(heavy_load, number // 4), named(common, number - number // 4 - 1))
    mixed = jax.random.permutation(jax.random.fold_in(own, 3), number_of)
    giver, sink = mixed[0:number_of // 2 * 2:2], mixed[1:number_of // 2 * 2:2]
    room = jnp.minimum(lengths[giver] - 1, bound - lengths[sink]) // 2
    room = jnp.where((giver == order[0]) | (sink == order[0]) | (lengths[sink] == 0), 0, jnp.maximum(room, 0))
    moved = jax.random.randint(jax.random.fold_in(own, 4), (number_of // 2,), 0, 1 << 20) % (room + 1)
    lengths = lengths.at[giver].add(-moved).at[sink].add(moved)
    labels = jnp.searchsorted(jnp.cumsum(lengths), jnp.arange(rows * top), side="right").astype(jnp.int32)
    grid = labels.reshape(top, rows).T
    grid = grid[jax.random.permutation(jax.random.fold_in(own, 1), rows)]
    rotation = jax.random.randint(jax.random.fold_in(own, 2), (rows, 1), 0, top)
    return jnp.take_along_axis(grid, (jnp.arange(top)[None, :] + rotation) % top, axis=1)


def load_shares(number_of, total, reach, lean, full):
    loads = [(1 << 20) // math.isqrt(standing ** lean) + 1 for standing in range(1, number_of + 1)]
    largest = reach if full else min(reach, max(-(-total // number_of), total * loads[0] // sum(loads)))
    least = 1 if total - largest >= number_of - 1 else 0
    given, surplus = [largest] + [least] * (number_of - 1), total - largest - least * (number_of - 1)
    while surplus > 0:
        candidates = [i for i in range(1, number_of) if given[i] < largest] or [i for i in range(1, number_of) if given[i] < reach]
        pool, left = sum([loads[i] for i in candidates]), surplus
        for i in candidates:
            addition = min(reach - given[i], max(1, left * loads[i] // pool), surplus)
            given[i] = given[i] + addition
            surplus = surplus - addition
    return np.array(given)


def centred(stream_key, extent, scale, limit, shards=(), held_as=jnp.bfloat16):
    factor_of = levels(stream_key, extent, shards, -0.22, 0.18) if shards else 1.0
    array = jax.random.normal(stream_key, extent, jnp.float32) * scale * factor_of
    return jnp.minimum(jnp.maximum(array, -limit), limit).astype(held_as)


def setup_inputs(seed: int = 0) -> dict:
    arg_keys = jax.random.split(jax.random.key(seed), 11)
    direction = centred(arg_keys[0], (3, NX, NY, NZ), 1.0, 6.0, ((1, 8), (2, 16)), jnp.float32)
    wind = centred(arg_keys[1], (3, NX, NY, NZ), 1.0, 5.0, ((1, 8), (2, 16)), jnp.float32)
    wind_gradient = centred(arg_keys[2], (9, NX, NY, NZ), 0.5, 3.0, ((1, 8), (2, 16)), jnp.float32)
    viscosity = jnp.clip(0.1 + 0.4 * jax.random.uniform(arg_keys[3], (NX, NY, NZ), jnp.float32) ** levels(arg_keys[3], (NX, NY, NZ), ((0, 8), (1, 16)), -0.2, 0.2), 0.1, 0.5)
    sample_owner_keys = jax.random.split(jax.random.fold_in(arg_keys[4], 1), N_TRACK * N_CROSS * S_DEV // S_DEV)
    sample_owner_turns = jax.random.permutation(jax.random.fold_in(arg_keys[4], 3), N_TRACK * N_CROSS * S_DEV // S_DEV)
    sample_owner = jax.vmap(lambda own, number: deal_out(jax.random.fold_in(arg_keys[4], 2), own, number, S_DEV, OWNERS, 1, CAP, 2))(sample_owner_keys, sample_owner_turns).reshape((N_TRACK, N_CROSS, S_DEV, 1))
    sample_cell = place_ends(jax.random.randint(arg_keys[5], (N_TRACK, N_CROSS, S_DEV), 0, CX * CY * NZ), jax.random.fold_in(arg_keys[5], 1), 0, (CX * CY * NZ) - 1).astype(jnp.int32)
    sample_gate = place_ends(jax.random.randint(arg_keys[6], (N_TRACK, N_CROSS, S_DEV), 0, OBS_DEV), jax.random.fold_in(arg_keys[6], 1), 0, OBS_DEV - 1).astype(jnp.int32)
    sight = centred(arg_keys[7], (3, OWNERS, OBS_DEV), 0.25, 1.5, ((1, 128),), jnp.float32)
    gate_counts = jax.vmap(lambda own: uneven(own, BEAMS, 3 * BEAMS * GATES // 4, GATES, 2))(jax.random.split(arg_keys[8], OWNERS)).reshape((OWNERS, BEAMS)).astype(jnp.int32)
    precision = draw_precision(jax.random.fold_in(arg_keys[10], 71), 0)
    return {"direction": direction, "wind": wind, "wind_gradient": wind_gradient, "viscosity": viscosity, "sample_owner": sample_owner, "sample_cell": sample_cell, "sample_gate": sample_gate, "sight": sight, "gate_counts": gate_counts, "precision": precision}


time_step = 0.2


def central(field, axis):
    widths = [(0, 0)] * field.ndim
    widths[axis] = (1, 1)
    padded = jnp.pad(field, widths)
    upper = lax.slice_in_dim(padded, 2, field.shape[axis] + 2, axis=axis)
    lower = lax.slice_in_dim(padded, 0, field.shape[axis], axis=axis)
    return (upper - lower) * 0.5


def neighbours(field):
    total = jnp.zeros_like(field)
    for axis in range(1, 4):
        widths = [(0, 0)] * field.ndim
        widths[axis] = (1, 1)
        padded = jnp.pad(field, widths)
        total = total + lax.slice_in_dim(padded, 2, field.shape[axis] + 2, axis=axis)
        total = total + lax.slice_in_dim(padded, 0, field.shape[axis], axis=axis)
    return total


def tangent_step(field, wind, grad, visc):
    adv = wind[0] * central(field, 1) + wind[1] * central(field, 2) + wind[2] * central(field, 3)
    gq = jnp.stack([grad[3 * i] * field[0] + grad[3 * i + 1] * field[1] + grad[3 * i + 2] * field[2] for i in range(3)])
    return field + time_step * (-adv - gq + visc * (neighbours(field) - 6.0 * field))


def adjoint_step(field, wind, grad, visc):
    moved = central(wind[0] * field, 1) + central(wind[1] * field, 2) + central(wind[2] * field, 3)
    gtr = jnp.stack([grad[j] * field[0] + grad[3 + j] * field[1] + grad[6 + j] * field[2] for j in range(3)])
    mixed = visc * field
    return field + time_step * (moved - gtr + neighbours(mixed) - 6.0 * mixed)


def reference(direction, wind, wind_gradient, viscosity, sample_owner, sample_cell, sample_gate, sight, gate_counts, precision):
    n_track, n_cross, s_dev = sample_cell.shape
    owning_ranks = n_track * n_cross
    cx = direction.shape[1] // n_track
    cy = direction.shape[2] // n_cross
    nz = direction.shape[3]
    obs = sight.shape[2]
    tangent = tangent_step(direction, wind, wind_gradient, viscosity)
    tile_x = jnp.arange(n_track, dtype=jnp.int32)[:, None, None]
    tile_y = jnp.arange(n_cross, dtype=jnp.int32)[None, :, None]
    gx = (tile_x * cx + sample_cell // (cy * nz)).reshape(-1)
    gy = (tile_y * cy + (sample_cell // nz) % cy).reshape(-1)
    gz = (sample_cell % nz).reshape(-1)
    owner = sample_owner.reshape(-1)
    gate = sample_gate.reshape(-1)
    values = tangent[:, gx, gy, gz]
    weights = sight[:, owner, gate]
    proj = jnp.sum(weights * values, axis=0)
    flat = owner * obs + gate
    observed = jnp.zeros((owning_ranks * obs,), jnp.float32).at[flat].add(proj)
    observed = observed.reshape(owning_ranks, BEAMS, GATES)
    live = (jnp.arange(GATES, dtype=jnp.int32)[None, None, :] < gate_counts[:, :, None]).astype(jnp.float32)
    weighted = jnp.einsum("dbg,dgh->dbh", live * observed, precision, precision=lax.Precision.HIGHEST) * live
    weighted = weighted.reshape(owning_ranks, obs)
    back = weights * weighted.reshape(-1)[flat][None, :]
    pulled = jnp.zeros_like(direction).at[:, gx, gy, gz].add(back)
    result = adjoint_step(pulled, wind, wind_gradient, viscosity)
    return result, weighted
```

```python
import functools

import jax
import jax.numpy as jnp
from jax import lax
from jax.experimental import pallas as pl
from jax.experimental.pallas import tpu as pltpu
from jax.sharding import PartitionSpec as P

time_step = 0.2
highest = lax.Precision.HIGHEST
tile = 256
lanes = 128
f32 = jnp.float32
bf16 = jnp.bfloat16
i32 = jnp.int32


def split(value):
    head = value.astype(bf16)
    return head, (value - head.astype(f32)).astype(bf16)


def rows_equal(count, row):
    iota = lax.broadcasted_iota(i32, (count, row.shape[1]), 0)
    return iota == row


def pick(mask, value):
    return jnp.sum(jnp.where(mask, value, 0.0), axis=0, keepdims=True)


def ones_at(mask):
    return jnp.where(mask, 1.0, 0.0).astype(bf16)


def dot_nt(a, b):
    return lax.dot_general(a, b, (((1,), (1,)), ((), ())), preferred_element_type=f32)


def dot_nn(a, b):
    return jnp.dot(a, b, preferred_element_type=f32)


def walk_tiles(first_ref, pointer, limit, tiles, visit):
    def first(p):
        return first_ref[jnp.minimum(p, tiles - 1) * tile]

    def go_on(carry):
        p, go = carry
        return go & (p < tiles) & (first(p) < limit)

    def step(carry):
        p, _ = carry
        visit(p)
        done = first_ref[p * tile + tile - 1] < limit
        return jnp.where(done, p + 1, p), done

    p, _ = lax.while_loop(go_on, step, (pointer[0], jnp.bool_(True)))
    pointer[0] = p


def sample_kernel(
    cell_s,
    field_ref,
    xlo_ref,
    xhi_ref,
    ylo_ref,
    yhi_ref,
    wind_ref,
    grad_ref,
    visc_ref,
    cell_ref,
    og_ref,
    slots_ref,
    rank_ref,
    plane_ref,
    value_ref,
    offset_ref,
    upper_ref,
    total_ref,
    pointer,
    *,
    obs,
):
    x = pl.program_id(0)
    nx = pl.num_programs(0)
    cy, nz = field_ref.shape[2], field_ref.shape[3]
    tiles = cell_ref.shape[0]
    owners = slots_ref.shape[0]
    per_step = -(-tiles // field_ref.shape[1])

    @pl.when(x == 0)
    def _():
        pointer[0] = 0
        value_ref[...] = jnp.zeros_like(value_ref)
        offset_ref[...] = jnp.zeros_like(offset_ref)
        a = lax.broadcasted_iota(i32, (tile, 2 * tile), 0)
        b = lax.broadcasted_iota(i32, (tile, 2 * tile), 1)
        upper_ref[...] = ones_at((a < b) | (b >= tile))

    y_at = lax.broadcasted_iota(i32, (cy, nz), 0)
    z_at = lax.broadcasted_iota(i32, (cy, nz), 1)
    visc = visc_ref[0]
    here = [field_ref[c, x] for c in range(3)]
    below = jnp.maximum(x - 1, 0)
    above = jnp.minimum(x + 1, nx - 1)
    for c in range(3):
        f = here[c]
        down = jnp.where(x == 0, xlo_ref[c], field_ref[c, below])
        up = jnp.where(x == nx - 1, xhi_ref[c], field_ref[c, above])
        left = jnp.where(y_at == 0, ylo_ref[c, pl.ds(x, 1), :], pltpu.roll(f, 1, 0))
        right = jnp.where(y_at == cy - 1, yhi_ref[c, pl.ds(x, 1), :], pltpu.roll(f, cy - 1, 0))
        under = jnp.where(z_at == 0, 0.0, pltpu.roll(f, 1, 1))
        over = jnp.where(z_at == nz - 1, 0.0, pltpu.roll(f, nz - 1, 1))
        adv = 0.5 * (
            wind_ref[0, 0] * (up - down) + wind_ref[1, 0] * (right - left) + wind_ref[2, 0] * (over - under)
        )
        gq = (
            grad_ref[3 * c, 0] * here[0]
            + grad_ref[3 * c + 1, 0] * here[1]
            + grad_ref[3 * c + 2, 0] * here[2]
        )
        near = up + down + right + left + over + under
        tangent = f + time_step * (visc * (near - 6.0 * f) - adv - gq)
        head, rest = split(tangent)
        plane_ref[c * cy : (c + 1) * cy, :nz] = head
        plane_ref[c * cy : (c + 1) * cy, nz:] = rest

    for k in range(per_step):
        t = x * per_step + k

        @pl.when(t < tiles)
        def _():
            mask = rows_equal(owners, og_ref[pl.ds(t, 1), :] // obs)
            counts = dot_nn(ones_at(mask), upper_ref[...])
            rank = pick(mask, counts[:, :tile] + offset_ref[...])
            rank_ref[pl.ds(t, 1), :] = rank.astype(i32)
            offset_ref[...] += counts[:, tile:]

    def visit(p):
        cells = cell_ref[pl.ds(p, 1), :]
        zs = ones_at(rows_equal(nz, cells % nz))
        line = cells // nz
        mask = rows_equal(cy, line - x * cy)
        found = dot_nn(plane_ref[...], jnp.concatenate([zs, zs], axis=0))
        for c in range(3):
            value_ref[c, pl.ds(p, 1), :] += pick(mask, found[c * cy : (c + 1) * cy])

    walk_tiles(cell_s, pointer, (x + 1) * cy * nz, tiles, visit)

    @pl.when(x == nx - 1)
    def _():
        total_ref[...] = jnp.zeros_like(total_ref)

        def add_tile(t, carry):
            og = og_ref[pl.ds(t, 1), :]
            mask = rows_equal(owners, og // obs)
            gate = og % obs
            ranks = ones_at(rows_equal(lanes, rank_ref[pl.ds(t, 1), :]))
            parts = []
            for c in range(3):
                head, rest = split(value_ref[c, pl.ds(t, 1), :])
                parts.append((head.astype(f32), rest.astype(f32)))
            low = gate % lanes
            parts.append(((gate - low).astype(f32), low.astype(f32)))
            left = jnp.concatenate(
                [
                    jnp.concatenate([jnp.where(mask, a, 0.0).astype(bf16), jnp.where(mask, b, 0.0).astype(bf16)], axis=1)
                    for a, b in parts
                ],
                axis=0,
            )
            total_ref[...] += dot_nt(left, jnp.concatenate([ranks, ranks], axis=1))
            return carry

        lax.fori_loop(0, tiles, add_tile, 0)
        for c in range(4):
            slots_ref[:, c, :] = total_ref[c * owners : (c + 1) * owners]


def owner_kernel(counts_s, got_ref, sight_ref, precision_ref, back_ref, weighted_ref, gate_ref):
    sources = got_ref.shape[0]
    group = 8
    wide = group * lanes
    beams = counts_s.shape[1]

    def gathered(i):
        return jnp.concatenate([got_ref[i * group + j] for j in range(group)], axis=1)

    def beam_mask(gate):
        return rows_equal(beams, gate // lanes)

    def collect(i, acc):
        rows = gathered(i)
        gate = rows[3:4].astype(i32)
        gates = ones_at(rows_equal(lanes, gate % lanes))
        gate_ref[i] = gates
        mask = beam_mask(gate)
        parts = []
        for k in range(3):
            head, rest = split(rows[k : k + 1])
            parts.append(jnp.where(mask, head.astype(f32), 0.0))
            parts.append(jnp.where(mask, rest.astype(f32), 0.0))
        left = jnp.concatenate(parts, axis=0).astype(bf16)
        return acc + dot_nt(left, gates)

    acc = lax.fori_loop(0, sources // group, collect, jnp.zeros((6 * beams, lanes), f32))
    sights = [
        jnp.concatenate([sight_ref[k, :, b * lanes : (b + 1) * lanes] for b in range(beams)], axis=0)
        for k in range(3)
    ]
    observed = jnp.zeros((beams, lanes), f32)
    for k in range(3):
        at = 2 * k * beams
        observed += sights[k] * (acc[at : at + beams] + acc[at + beams : at + 2 * beams])
    beam_at = lax.broadcasted_iota(i32, (beams, lanes), 0)
    gate_at = lax.broadcasted_iota(i32, (beams, lanes), 1)
    limit = jnp.zeros((beams, lanes), i32)
    for b in range(beams):
        limit = jnp.where(beam_at == b, counts_s[0, b], limit)
    live = jnp.where(gate_at < limit, 1.0, 0.0)
    weighted = live * jnp.dot(live * observed, precision_ref[0], precision=highest, preferred_element_type=f32)
    for b in range(beams):
        weighted_ref[:, b * lanes : (b + 1) * lanes] = weighted[b : b + 1]
    spread = jnp.concatenate([s * weighted for s in sights], axis=0)
    head = spread.astype(bf16).astype(f32)
    table = jnp.concatenate([head, spread - head], axis=1).astype(bf16)

    def give(i, carry):
        gate = gathered(i)[3:4].astype(i32)
        mask = beam_mask(gate)
        gates = gate_ref[i]
        found = dot_nn(table, jnp.concatenate([gates, gates], axis=0))
        rows = jnp.concatenate(
            [pick(mask, found[k * beams : (k + 1) * beams]) for k in range(3)] + [jnp.zeros((1, wide), f32)], axis=0
        )
        for j in range(group):
            back_ref[i * group + j] = rows[:, j * lanes : (j + 1) * lanes]
        return carry

    lax.fori_loop(0, sources // group, give, 0)


def adjoint_kernel(
    cell_s,
    back_ref,
    cell_ref,
    og_ref,
    rank_ref,
    wind_ref,
    grad_ref,
    visc_ref,
    out_ref,
    xlo_ref,
    xhi_ref,
    ylo_ref,
    yhi_ref,
    table_ref,
    value_ref,
    plane_ref,
    carry_ref,
    passed_ref,
    pointer,
    *,
    obs,
):
    x = pl.program_id(0)
    nx = pl.num_programs(0) - 1
    cy, nz = out_ref.shape[2], out_ref.shape[3]
    tiles = cell_ref.shape[0]
    owners = back_ref.shape[0]

    @pl.when(x == 0)
    def _():
        pointer[0] = 0
        for c in range(3):
            head, rest = split(back_ref[:, c, :])
            table_ref[c * owners : (c + 1) * owners, :lanes] = head
            table_ref[c * owners : (c + 1) * owners, lanes:] = rest
        carry_ref[...] = jnp.zeros_like(carry_ref)
        passed_ref[...] = jnp.zeros_like(passed_ref)

        def restore(t, carry):
            mask = rows_equal(owners, og_ref[pl.ds(t, 1), :] // obs)
            ranks = ones_at(rows_equal(lanes, rank_ref[pl.ds(t, 1), :]))
            found = dot_nn(table_ref[...], jnp.concatenate([ranks, ranks], axis=0))
            for c in range(3):
                value_ref[c, pl.ds(t, 1), :] = pick(mask, found[c * owners : (c + 1) * owners])
            return carry

        lax.fori_loop(0, tiles, restore, 0)

    @pl.when(x < nx)
    def _():
        plane_ref[...] = jnp.zeros_like(plane_ref)

        def visit(p):
            cells = cell_ref[pl.ds(p, 1), :]
            zs = ones_at(rows_equal(nz, cells % nz))
            mask = rows_equal(cy, cells // nz - x * cy)
            heads, rests = [], []
            for c in range(3):
                head, rest = split(value_ref[c, pl.ds(p, 1), :])
                heads.append(jnp.where(mask, head.astype(f32), 0.0).astype(bf16))
                rests.append(jnp.where(mask, rest.astype(f32), 0.0).astype(bf16))
            left = jnp.concatenate([jnp.concatenate(heads, axis=0), jnp.concatenate(rests, axis=0)], axis=1)
            plane_ref[...] += dot_nt(left, jnp.concatenate([zs, zs], axis=1))

        walk_tiles(cell_s, pointer, (x + 1) * cy * nz, tiles, visit)

        y_at = lax.broadcasted_iota(i32, (cy, nz), 0)
        z_at = lax.broadcasted_iota(i32, (cy, nz), 1)
        visc = visc_ref[0]
        pulled = [plane_ref[c * cy : (c + 1) * cy] for c in range(3)]
        for c in range(3):
            p = pulled[c]
            mixed = visc * p
            sx = 0.5 * wind_ref[0, 0] * p
            sy = 0.5 * wind_ref[1, 0] * p
            sz = 0.5 * wind_ref[2, 0] * p
            to_down = mixed + sx
            to_up = mixed - sx
            to_left = mixed + sy
            to_right = mixed - sy
            to_under = mixed + sz
            to_over = mixed - sz
            gtr = grad_ref[c, 0] * pulled[0] + grad_ref[3 + c, 0] * pulled[1] + grad_ref[6 + c, 0] * pulled[2]
            around = (
                jnp.where(y_at == cy - 1, 0.0, pltpu.roll(to_left, cy - 1, 0))
                + jnp.where(y_at == 0, 0.0, pltpu.roll(to_right, 1, 0))
                + jnp.where(z_at == nz - 1, 0.0, pltpu.roll(to_under, nz - 1, 1))
                + jnp.where(z_at == 0, 0.0, pltpu.roll(to_over, 1, 1))
            )
            own = p + time_step * (around - gtr - 6.0 * mixed)
            out_ref[c, 0] = carry_ref[c] + time_step * to_down
            carry_ref[c] = own + passed_ref[c]
            passed_ref[c] = time_step * to_up
            ylo_ref[c, pl.ds(x, 1), :] = time_step * to_left[0:1]
            yhi_ref[c, pl.ds(x, 1), :] = time_step * to_right[cy - 1 : cy]

            @pl.when(x == 0)
            def _():
                xlo_ref[c] = time_step * to_down

            @pl.when(x == nx - 1)
            def _():
                xhi_ref[c] = time_step * to_up

    @pl.when(x == nx)
    def _():
        out_ref[:, 0] = carry_ref[...]


def edge_kernel(
    given_ref, xlo_ref, xhi_ref, ylo_ref, yhi_ref, out_ref, low_ref, high_ref, left_ref, right_ref, sems
):
    del given_ref
    nx, cy = out_ref.shape[1], out_ref.shape[2]
    inner = nx - 2
    places = [
        (out_ref.at[:, 0], low_ref),
        (out_ref.at[:, nx - 1], high_ref),
        (out_ref.at[:, pl.ds(1, inner), pl.ds(0, 8)], left_ref),
        (out_ref.at[:, pl.ds(1, inner), pl.ds(cy - 8, 8)], right_ref),
    ]
    reads = [pltpu.make_async_copy(a, b, sems.at[i]) for i, (a, b) in enumerate(places)]
    for read in reads:
        read.start()
    writes = [pltpu.make_async_copy(b, a, sems.at[4 + i]) for i, (a, b) in enumerate(places)]
    for i, (x, ref, halo) in enumerate(((0, low_ref, xlo_ref), (nx - 1, high_ref, xhi_ref))):
        reads[i].wait()
        ref[...] += halo[...]
        ref[:, 0:1, :] += ylo_ref[:, x : x + 1, :]
        ref[:, cy - 1 : cy, :] += yhi_ref[:, x : x + 1, :]
        writes[i].start()
    reads[2].wait()
    for k in range(inner):
        left_ref[:, k, 0:1, :] += ylo_ref[:, k + 1 : k + 2, :]
    writes[2].start()
    reads[3].wait()
    for k in range(inner):
        right_ref[:, k, 7:8, :] += yhi_ref[:, k + 1 : k + 2, :]
    writes[3].start()
    for write in writes:
        write.wait()


def shifted(value, axis, by):
    count = lax.axis_size(axis)
    return lax.ppermute(value, axis, [(i, i + by) for i in range(count) if 0 <= i + by < count])


def whole(shape):
    return pl.BlockSpec(shape, lambda *_: (0,) * len(shape))


def body(
    direction,
    wind,
    wind_gradient,
    viscosity,
    sample_owner,
    sample_cell,
    sample_gate,
    sight,
    gate_counts,
    precision,
):
    _, cx, cy, nz = direction.shape
    owners = lax.axis_size("track") * lax.axis_size("cross")
    obs = sight.shape[2]
    samples = sample_cell.shape[2]
    tiles = samples // tile
    names = ("track", "cross")
    big = pltpu.CompilerParams(dimension_semantics=("arbitrary",), vmem_limit_bytes=48 << 20)

    xlo = shifted(direction[:, cx - 1], "track", 1)
    xhi = shifted(direction[:, 0], "track", -1)
    ylo = shifted(direction[:, :, cy - 1], "cross", 1)
    yhi = shifted(direction[:, :, 0], "cross", -1)
    cells, og = lax.sort(
        (sample_cell.reshape(-1), sample_owner.reshape(-1) * obs + sample_gate.reshape(-1)), num_keys=1, is_stable=False
    )
    cell_rows = cells.reshape(tiles, tile)
    og_rows = og.reshape(tiles, tile)

    def plane(count, last):
        return pl.BlockSpec((count, 1, cy, nz), lambda x, *_: (0, jnp.minimum(x, last), 0, 0))

    def visc_plane(last):
        return pl.BlockSpec((1, cy, nz), lambda x, *_: (jnp.minimum(x, last), 0, 0))

    rows = whole((tiles, tile))
    slots, rank_rows = pl.pallas_call(
        functools.partial(sample_kernel, obs=obs),
        name="sample",
        grid_spec=pltpu.PrefetchScalarGridSpec(
            num_scalar_prefetch=1,
            grid=(cx,),
            in_specs=[
                whole((3, cx, cy, nz)),
                whole((3, cy, nz)),
                whole((3, cy, nz)),
                whole((3, cx, nz)),
                whole((3, cx, nz)),
                plane(3, cx - 1),
                plane(9, cx - 1),
                visc_plane(cx - 1),
                rows,
                rows,
            ],
            out_specs=[whole((owners, 4, lanes)), rows],
            scratch_shapes=[
                pltpu.VMEM((3 * cy, 2 * nz), bf16),
                pltpu.VMEM((3, tiles, tile), f32),
                pltpu.VMEM((owners, tile), f32),
                pltpu.VMEM((tile, 2 * tile), bf16),
                pltpu.VMEM((4 * owners, lanes), f32),
                pltpu.SMEM((1,), i32),
            ],
        ),
        out_shape=[
            jax.ShapeDtypeStruct((owners, 4, lanes), f32),
            jax.ShapeDtypeStruct((tiles, tile), i32),
        ],
        compiler_params=big,
    )(cells, direction, xlo, xhi, ylo, yhi, wind, wind_gradient, viscosity, cell_rows, og_rows)

    got = lax.all_to_all(slots, names, split_axis=0, concat_axis=0, tiled=True)
    back, weighted = pl.pallas_call(
        owner_kernel,
        name="owner",
        in_specs=[
            pl.BlockSpec(memory_space=pltpu.SMEM),
            pl.BlockSpec(memory_space=pltpu.VMEM),
            pl.BlockSpec(memory_space=pltpu.VMEM),
            pl.BlockSpec(memory_space=pltpu.VMEM),
        ],
        out_specs=[pl.BlockSpec(memory_space=pltpu.VMEM), pl.BlockSpec(memory_space=pltpu.VMEM)],
        scratch_shapes=[pltpu.VMEM((owners // 8, lanes, 8 * lanes), bf16)],
        out_shape=[
            jax.ShapeDtypeStruct((owners, 4, lanes), f32),
            jax.ShapeDtypeStruct((1, obs), f32),
        ],
        compiler_params=pltpu.CompilerParams(vmem_limit_bytes=48 << 20),
    )(gate_counts, got, sight, precision)
    returned = lax.all_to_all(back, names, split_axis=0, concat_axis=0, tiled=True)

    result, sent_xlo, sent_xhi, sent_ylo, sent_yhi = pl.pallas_call(
        functools.partial(adjoint_kernel, obs=obs),
        name="adjoint",
        grid_spec=pltpu.PrefetchScalarGridSpec(
            num_scalar_prefetch=1,
            grid=(cx + 1,),
            in_specs=[
                whole((owners, 4, lanes)),
                rows,
                rows,
                rows,
                plane(3, cx - 1),
                plane(9, cx - 1),
                visc_plane(cx - 1),
            ],
            out_specs=[
                pl.BlockSpec((3, 1, cy, nz), lambda x, *_: (0, jnp.maximum(x - 1, 0), 0, 0)),
                whole((3, cy, nz)),
                whole((3, cy, nz)),
                whole((3, cx, nz)),
                whole((3, cx, nz)),
            ],
            scratch_shapes=[
                pltpu.VMEM((3 * owners, 2 * lanes), bf16),
                pltpu.VMEM((3, tiles, tile), f32),
                pltpu.VMEM((3 * cy, nz), f32),
                pltpu.VMEM((3, cy, nz), f32),
                pltpu.VMEM((3, cy, nz), f32),
                pltpu.SMEM((1,), i32),
            ],
        ),
        out_shape=[
            jax.ShapeDtypeStruct((3, cx, cy, nz), f32),
            jax.ShapeDtypeStruct((3, cy, nz), f32),
            jax.ShapeDtypeStruct((3, cy, nz), f32),
            jax.ShapeDtypeStruct((3, cx, nz), f32),
            jax.ShapeDtypeStruct((3, cx, nz), f32),
        ],
        compiler_params=big,
    )(cells, returned, cell_rows, og_rows, rank_rows, wind, wind_gradient, viscosity)

    from_low = shifted(sent_xhi, "track", 1)
    from_high = shifted(sent_xlo, "track", -1)
    from_left = shifted(sent_yhi, "cross", 1)
    from_right = shifted(sent_ylo, "cross", -1)
    vmem = pl.BlockSpec(memory_space=pltpu.VMEM)
    hbm = pl.BlockSpec(memory_space=pl.ANY)
    result = pl.pallas_call(
        edge_kernel,
        name="edges",
        in_specs=[hbm, vmem, vmem, vmem, vmem],
        out_specs=hbm,
        scratch_shapes=[
            pltpu.VMEM((3, cy, nz), f32),
            pltpu.VMEM((3, cy, nz), f32),
            pltpu.VMEM((3, cx - 2, 8, nz), f32),
            pltpu.VMEM((3, cx - 2, 8, nz), f32),
            pltpu.SemaphoreType.DMA((8,)),
        ],
        out_shape=jax.ShapeDtypeStruct((3, cx, cy, nz), f32),
        input_output_aliases={0: 0},
        compiler_params=pltpu.CompilerParams(vmem_limit_bytes=48 << 20),
    )(result, from_low, from_high, from_left, from_right)
    return (result, weighted)


def solution(mesh):
    placed = (
        P(None, "track", "cross", None),
        P(None, "track", "cross", None),
        P(None, "track", "cross", None),
        P("track", "cross", None),
        P("track", "cross", None, None),
        P("track", "cross", None),
        P("track", "cross", None),
        P(None, ("track", "cross"), None),
        P(("track", "cross"), None),
        P(("track", "cross"), None, None),
    )
    return jax.shard_map(
        body,
        mesh=mesh,
        in_specs=placed,
        out_specs=(P(None, "track", "cross", None), P(("track", "cross"), None)),
        check_vma=False,
    )
```

```python
import functools

import jax
import jax.numpy as jnp
from jax import lax
from jax.experimental import pallas as pl
from jax.experimental.pallas import tpu as pltpu
from jax.sharding import PartitionSpec as P

time_step = 0.2
highest = lax.Precision.HIGHEST
tile = 256
lanes = 128
span = 64
strip = 16
batch = 4
row_bits = 8
f32 = jnp.float32
bf16 = jnp.bfloat16
i32 = jnp.int32


def split(value):
    head = value.astype(bf16)
    return head, (value - head.astype(f32)).astype(bf16)


def rows_equal(count, row):
    iota = lax.broadcasted_iota(i32, (count, row.shape[1]), 0)
    return iota == row


def pick(mask, value):
    return jnp.sum(jnp.where(mask, value, 0.0), axis=0, keepdims=True)


def onehot(count, row):
    iota = lax.broadcasted_iota(i32, (count, row.shape[1]), 0).astype(bf16)
    return jnp.where(iota == row.astype(f32).astype(bf16), jnp.ones((), bf16), jnp.zeros((), bf16))


def ones_at(mask):
    return jnp.where(mask, 1.0, 0.0).astype(bf16)


def dot_nt(a, b):
    return lax.dot_general(a, b, (((1,), (1,)), ((), ())), preferred_element_type=f32)


def dot_nn(a, b):
    return jnp.dot(a, b, preferred_element_type=f32)


def window(cell_s, t, rows):
    first = cell_s[t, 0] >> row_bits
    last = cell_s[t, tile - 1] >> row_bits
    base = jnp.minimum((first >> 4) << 4, rows - span)
    return pl.multiple_of(base, 16), last - base - span + 1


def each_tile(cell_s, tiles, rows, visit, more):
    def first(t, most):
        base, over = window(cell_s, t, rows)
        visit(t, base)
        return jnp.maximum(most, over)

    most = lax.fori_loop(0, tiles, first, i32(0), unroll=8)

    @pl.when(most > 0)
    def _():
        def rest(t, carry):
            base, over = window(cell_s, t, rows)

            def step(k, carry):
                least = base + k * span
                more(t, pl.multiple_of(jnp.minimum(least, rows - span), 16), least)
                return carry

            lax.fori_loop(1, 1 + (over + span - 1) // span, step, 0)
            return carry

        lax.fori_loop(0, tiles, rest, 0)


def slot_parts(slot):
    return slot // (2 * lanes), slot % (2 * lanes)


def sample_kernel(
    cell_s,
    field_hbm,
    xlo_ref,
    xhi_ref,
    ylo_ref,
    yhi_ref,
    wind_hbm,
    grad_hbm,
    visc_hbm,
    cell_ref,
    og_ref,
    slots_ref,
    slot_ref,
    field_ref,
    wind_ref,
    grad_ref,
    visc_ref,
    plane_ref,
    value_ref,
    offset_ref,
    upper_ref,
    total_ref,
    sems,
    *,
    obs,
):
    nx, cy, nz = visc_ref.shape
    tiles = cell_ref.shape[0]
    owners = 2 * slots_ref.shape[0]
    rows = nx * cy

    def copies(k):
        part = pl.ds(k * batch, batch)
        return [
            pltpu.make_async_copy(field_hbm.at[:, part], field_ref.at[:, pl.ds(k * batch + 1, batch)], sems.at[0, k]),
            pltpu.make_async_copy(wind_hbm.at[:, part], wind_ref.at[:, part], sems.at[1, k]),
            pltpu.make_async_copy(grad_hbm.at[:, part], grad_ref.at[:, part], sems.at[2, k]),
            pltpu.make_async_copy(visc_hbm.at[part], visc_ref.at[part], sems.at[3, k]),
        ]

    batches = nx // batch
    for k in range(batches):
        for copy in copies(k):
            copy.start()

    along, across = lax.axis_index("track"), lax.axis_index("cross")
    field_ref[:, 0] = jnp.where(along == 0, 0.0, xlo_ref[...])
    field_ref[:, nx + 1] = jnp.where(along == lax.axis_size("track") - 1, 0.0, xhi_ref[...])
    left_edge = across == 0
    right_edge = across == lax.axis_size("cross") - 1

    offset_ref[...] = jnp.zeros_like(offset_ref)
    a = lax.broadcasted_iota(i32, (tile, tile), 0)
    b = lax.broadcasted_iota(i32, (tile, tile), 1)
    upper_ref[...] = ones_at(a <= b)

    def rank(t, carry):
        own = og_ref[pl.ds(t, 1), :] // obs
        mask = rows_equal(owners, own)
        counts = dot_nn(ones_at(mask), upper_ref[...])
        offset = offset_ref[...]
        ranks = pick(mask, counts + jnp.concatenate([offset] * (tile // lanes), axis=1))
        slot_ref[pl.ds(t, 1), :] = own * lanes + ranks.astype(i32) - 1
        offset_ref[...] = offset + jnp.broadcast_to(counts[:, tile - 1 : tile], offset.shape)
        return carry

    lax.fori_loop(0, tiles, rank, 0, unroll=8)

    y_at = lax.broadcasted_iota(i32, (strip, nz), 0)
    z_at = lax.broadcasted_iota(i32, (strip, nz), 1)

    def advance(x, carry):
        for y in range(0, cy, strip):
            part = pl.ds(y, strip)
            visc = time_step * visc_ref[x, part]
            wind = [(-0.5 * time_step) * wind_ref[a, x, part] for a in range(3)]
            here = [field_ref[c, x + 1, part] for c in range(3)]
            for c in range(3):
                f = here[c]
                down = field_ref[c, x, part]
                up = field_ref[c, x + 2, part]
                if y == 0:
                    before = jnp.where(left_edge, 0.0, ylo_ref[c, pl.ds(x, 1), :])
                else:
                    before = field_ref[c, x + 1, y - 1 : y]
                if y + strip == cy:
                    after = jnp.where(right_edge, 0.0, yhi_ref[c, pl.ds(x, 1), :])
                else:
                    after = field_ref[c, x + 1, y + strip : y + strip + 1]
                left = jnp.where(y_at == 0, before, pltpu.roll(f, 1, 0))
                right = jnp.where(y_at == strip - 1, after, pltpu.roll(f, strip - 1, 0))
                under = jnp.where(z_at == 0, 0.0, pltpu.roll(f, 1, 1))
                over = jnp.where(z_at == nz - 1, 0.0, pltpu.roll(f, nz - 1, 1))
                near = (up + down) + (right + left) + (over + under)
                tangent = f + visc * (near - 6.0 * f)
                tangent += wind[0] * (up - down) + wind[1] * (right - left) + wind[2] * (over - under)
                gq = (
                    grad_ref[3 * c, x, part] * here[0]
                    + grad_ref[3 * c + 1, x, part] * here[1]
                    + grad_ref[3 * c + 2, x, part] * here[2]
                )
                head, rest = split(tangent - time_step * gq)
                at = pl.multiple_of(x * cy + y, strip)
                plane_ref[c, pl.ds(at, strip), :nz] = head
                plane_ref[c, pl.ds(at, strip), nz:] = rest
        return carry

    copies(0)[0].wait()
    for k in range(batches):
        for copy in copies(k)[1:]:
            copy.wait()
        if k + 1 < batches:
            copies(k + 1)[0].wait()
        lax.fori_loop(k * batch, (k + 1) * batch, advance, 0)

    def find(t, begin, least):
        cells = cell_ref[pl.ds(t, 1), :]
        zs = onehot(nz, cells % nz)
        line = cells // nz
        mask = rows_equal(span, jnp.where(line >= least, line - begin, -1))
        block = jnp.concatenate(
            [plane_ref[c, pl.ds(begin, span), h * nz : (h + 1) * nz] for h in range(2) for c in range(3)], axis=0
        )
        found = dot_nn(block, zs)
        found = found[: 3 * span] + found[3 * span :]
        return [pick(mask, found[c * span : (c + 1) * span]) for c in range(3)]

    def gather(t, begin):
        for c, value in enumerate(find(t, begin, 0)):
            value_ref[c, pl.ds(t, 1), :] = value

    def gather_more(t, begin, least):
        for c, value in enumerate(find(t, begin, least)):
            value_ref[c, pl.ds(t, 1), :] += value

    each_tile(cell_s, tiles, rows, gather, gather_more)

    total_ref[...] = jnp.zeros_like(total_ref)
    half = owners // 2

    def add_tile(t, carry):
        line, column = slot_parts(slot_ref[pl.ds(t, 1), :])
        gate = og_ref[pl.ds(t, 1), :] % obs
        mask = rows_equal(half, line)
        columns = onehot(2 * lanes, column)
        low = gate % lanes
        parts = []
        for c in range(3):
            head, rest = split(value_ref[c, pl.ds(t, 1), :])
            parts.append((head.astype(f32), rest.astype(f32)))
        parts.append(((gate - low).astype(f32), low.astype(f32)))
        left = jnp.concatenate(
            [
                jnp.concatenate([jnp.where(mask, a, 0.0).astype(bf16), jnp.where(mask, b, 0.0).astype(bf16)], axis=1)
                for a, b in parts
            ],
            axis=0,
        )
        total_ref[...] += dot_nt(left, jnp.concatenate([columns, columns], axis=1))
        return carry

    lax.fori_loop(0, tiles, add_tile, 0, unroll=8)
    for c in range(4):
        for h in range(2):
            slots_ref[:, h, c, :] = total_ref[c * half : (c + 1) * half, h * lanes : (h + 1) * lanes]


def owner_kernel(counts_s, got_ref, sight_ref, precision_ref, back_ref, weighted_ref, gate_ref):
    sources = got_ref.shape[0]
    group = 8
    wide = group * lanes
    beams = counts_s.shape[1]

    def gathered(i):
        return jnp.concatenate([got_ref[i * group + j] for j in range(group)], axis=1)

    def beam_mask(gate):
        return rows_equal(beams, gate // lanes)

    def collect(i, acc):
        rows = gathered(i)
        gate = rows[3:4].astype(i32)
        gates = ones_at(rows_equal(lanes, gate % lanes))
        gate_ref[i] = gates
        mask = beam_mask(gate)
        parts = []
        for k in range(3):
            head, rest = split(rows[k : k + 1])
            parts.append(jnp.where(mask, head.astype(f32), 0.0))
            parts.append(jnp.where(mask, rest.astype(f32), 0.0))
        left = jnp.concatenate(parts, axis=0).astype(bf16)
        return acc + dot_nt(left, gates)

    acc = lax.fori_loop(0, sources // group, collect, jnp.zeros((6 * beams, lanes), f32), unroll=4)
    sights = [
        jnp.concatenate([sight_ref[k, :, b * lanes : (b + 1) * lanes] for b in range(beams)], axis=0)
        for k in range(3)
    ]
    observed = jnp.zeros((beams, lanes), f32)
    for k in range(3):
        at = 2 * k * beams
        observed += sights[k] * (acc[at : at + beams] + acc[at + beams : at + 2 * beams])
    beam_at = lax.broadcasted_iota(i32, (beams, lanes), 0)
    gate_at = lax.broadcasted_iota(i32, (beams, lanes), 1)
    limit = jnp.zeros((beams, lanes), i32)
    for b in range(beams):
        limit = jnp.where(beam_at == b, counts_s[0, b], limit)
    live = jnp.where(gate_at < limit, 1.0, 0.0)
    weighted = live * jnp.dot(live * observed, precision_ref[0], precision=highest, preferred_element_type=f32)
    for b in range(beams):
        weighted_ref[:, b * lanes : (b + 1) * lanes] = weighted[b : b + 1]
    spread = jnp.concatenate([s * weighted for s in sights], axis=0)
    head = spread.astype(bf16).astype(f32)
    table = jnp.concatenate([head, spread - head], axis=1).astype(bf16)

    def give(i, carry):
        gate = gathered(i)[3:4].astype(i32)
        mask = beam_mask(gate)
        gates = gate_ref[i]
        found = dot_nn(table, jnp.concatenate([gates, gates], axis=0))
        rows = jnp.concatenate(
            [pick(mask, found[k * beams : (k + 1) * beams]) for k in range(3)] + [jnp.zeros((1, wide), f32)], axis=0
        )
        for j in range(group):
            back_ref[i * group + j] = rows[:, j * lanes : (j + 1) * lanes]
        return carry

    lax.fori_loop(0, sources // group, give, 0, unroll=4)


def adjoint_kernel(
    cell_s,
    back_ref,
    cell_ref,
    slot_ref,
    wind_hbm,
    grad_hbm,
    visc_hbm,
    out_hbm,
    xlo_ref,
    xhi_ref,
    ylo_ref,
    yhi_ref,
    wind_ref,
    grad_ref,
    visc_ref,
    table_ref,
    value_ref,
    plane_ref,
    out_ref,
    sems,
):
    nx, cy, nz = visc_ref.shape
    tiles = cell_ref.shape[0]
    half = back_ref.shape[0]
    rows = nx * cy

    copies = [
        pltpu.make_async_copy(wind_hbm, wind_ref, sems.at[0, 0]),
        pltpu.make_async_copy(grad_hbm, grad_ref, sems.at[1, 0]),
        pltpu.make_async_copy(visc_hbm, visc_ref, sems.at[2, 0]),
    ]

    def write(x):
        return pltpu.make_async_copy(out_ref.at[:, x + 1], out_hbm.at[:, x], sems.at[3, x])

    for copy in copies:
        copy.start()
    for c in range(3):
        for h in range(2):
            head, rest = split(back_ref[:, h, c, :])
            table_ref[c * half : (c + 1) * half, h * lanes : (h + 1) * lanes] = head
            table_ref[c * half : (c + 1) * half, (2 + h) * lanes : (3 + h) * lanes] = rest
    plane_ref[...] = jnp.zeros_like(plane_ref)

    def restore(t, carry):
        line, column = slot_parts(slot_ref[pl.ds(t, 1), :])
        mask = rows_equal(half, line)
        columns = onehot(2 * lanes, column)
        found = dot_nn(table_ref[...], jnp.concatenate([columns, columns], axis=0))
        for c in range(3):
            value_ref[c, pl.ds(t, 1), :] = pick(mask, found[c * half : (c + 1) * half])
        return carry

    lax.fori_loop(0, tiles, restore, 0, unroll=8)

    def put(t, begin, least):
        cells = cell_ref[pl.ds(t, 1), :]
        zs = onehot(nz, cells % nz)
        line = cells // nz
        mask = rows_equal(span, jnp.where(line >= least, line - begin, -1))
        heads, rests = [], []
        for c in range(3):
            head, rest = split(value_ref[c, pl.ds(t, 1), :])
            heads.append(jnp.where(mask, head.astype(f32), 0.0).astype(bf16))
            rests.append(jnp.where(mask, rest.astype(f32), 0.0).astype(bf16))
        left = jnp.concatenate([jnp.concatenate(heads, axis=0), jnp.concatenate(rests, axis=0)], axis=1)
        added = dot_nt(left, jnp.concatenate([zs, zs], axis=1))
        for c in range(3):
            plane_ref[c, pl.ds(begin, span), :] += added[c * span : (c + 1) * span]

    each_tile(cell_s, tiles, rows, lambda t, base: put(t, base, 0), put)

    y_at = lax.broadcasted_iota(i32, (strip, nz), 0)
    z_at = lax.broadcasted_iota(i32, (strip, nz), 1)
    strips = cy // strip

    def advance(x, carry):
        def give(k):
            part = pl.ds(k * strip, strip)
            at = pl.multiple_of(x * cy + k * strip, strip)
            pulled = [plane_ref[c, pl.ds(at, strip), :] for c in range(3)]
            visc = time_step * visc_ref[x, part]
            wind = (0.5 * time_step) * wind_ref[1, x, part]
            mixed = [visc * p for p in pulled]
            moved = [wind * p for p in pulled]
            return pulled, mixed, [m + w for m, w in zip(mixed, moved)], [m - w for m, w in zip(mixed, moved)]

        later = give(0)
        before = [0.0] * 3
        for k in range(strips):
            pulled, mixed, to_left, to_right = later
            part = pl.ds(k * strip, strip)
            after = [0.0] * 3
            if k + 1 < strips:
                later = give(k + 1)
                after = [v[0:1] for v in later[2]]
            wind_x = (0.5 * time_step) * wind_ref[0, x, part]
            wind_z = (0.5 * time_step) * wind_ref[2, x, part]
            for c in range(3):
                p = pulled[c]
                sx = wind_x * p
                sz = wind_z * p
                gtr = (
                    grad_ref[c, x, part] * pulled[0]
                    + grad_ref[3 + c, x, part] * pulled[1]
                    + grad_ref[6 + c, x, part] * pulled[2]
                )
                around = (
                    jnp.where(y_at == strip - 1, after[c], pltpu.roll(to_left[c], strip - 1, 0))
                    + jnp.where(y_at == 0, before[c], pltpu.roll(to_right[c], 1, 0))
                ) + (
                    jnp.where(z_at == nz - 1, 0.0, pltpu.roll(mixed[c] + sz, nz - 1, 1))
                    + jnp.where(z_at == 0, 0.0, pltpu.roll(mixed[c] - sz, 1, 1))
                )
                own = (p - 6.0 * mixed[c]) + (around - time_step * gtr)
                out_ref[c, x, part] += mixed[c] + sx
                out_ref[c, x + 1, part] += own
                out_ref[c, x + 2, part] = mixed[c] - sx
            if k == 0:
                for c in range(3):
                    ylo_ref[c, pl.ds(x, 1), :] = to_left[c][0:1]
            if k + 1 == strips:
                for c in range(3):
                    yhi_ref[c, pl.ds(x, 1), :] = to_right[c][strip - 1 : strip]
            before = [v[strip - 1 : strip] for v in to_right]

        @pl.when(x > 0)
        def _():
            write(x - 1).start()

        return carry

    for copy in copies:
        copy.wait()
    out_ref[:, 0:2] = jnp.zeros((3, 2, cy, nz), f32)
    lax.fori_loop(0, nx, advance, 0)
    xlo_ref[...] = out_ref[:, 0]
    xhi_ref[...] = out_ref[:, nx + 1]
    write(nx - 1).start()

    def end(x, carry):
        write(x).wait()
        return carry

    lax.fori_loop(0, nx, end, 0)


def edge_kernel(
    given_ref, xlo_ref, xhi_ref, ylo_ref, yhi_ref, out_ref, low_ref, high_ref, left_ref, right_ref, sems
):
    del given_ref
    along, across = lax.axis_index("track"), lax.axis_index("cross")
    last_along, last_across = lax.axis_size("track") - 1, lax.axis_size("cross") - 1
    ylo = jnp.where(across == 0, 0.0, ylo_ref[...])
    yhi = jnp.where(across == last_across, 0.0, yhi_ref[...])
    nx, cy = out_ref.shape[1], out_ref.shape[2]
    inner = nx - 2
    places = [
        (out_ref.at[:, 0], low_ref),
        (out_ref.at[:, nx - 1], high_ref),
        (out_ref.at[:, pl.ds(1, inner), pl.ds(0, 8)], left_ref),
        (out_ref.at[:, pl.ds(1, inner), pl.ds(cy - 8, 8)], right_ref),
    ]
    reads = [pltpu.make_async_copy(a, b, sems.at[i]) for i, (a, b) in enumerate(places)]
    for read in reads:
        read.start()
    writes = [pltpu.make_async_copy(b, a, sems.at[4 + i]) for i, (a, b) in enumerate(places)]
    for i, (x, ref, halo, edge) in enumerate(
        ((0, low_ref, xlo_ref, along == 0), (nx - 1, high_ref, xhi_ref, along == last_along))
    ):
        reads[i].wait()
        ref[...] += jnp.where(edge, 0.0, halo[...])
        ref[:, 0:1, :] += ylo[:, x : x + 1, :]
        ref[:, cy - 1 : cy, :] += yhi[:, x : x + 1, :]
        writes[i].start()
    reads[2].wait()
    for k in range(inner):
        left_ref[:, k, 0:1, :] += ylo[:, k + 1 : k + 2, :]
    writes[2].start()
    reads[3].wait()
    for k in range(inner):
        right_ref[:, k, 7:8, :] += yhi[:, k + 1 : k + 2, :]
    writes[3].start()
    for write in writes:
        write.wait()


def shifted(value, axis, by):
    count = lax.axis_size(axis)
    return lax.ppermute(value, axis, [(i, (i + by) % count) for i in range(count)])


vmem = pl.BlockSpec(memory_space=pltpu.VMEM)
smem = pl.BlockSpec(memory_space=pltpu.SMEM)
hbm = pl.BlockSpec(memory_space=pltpu.HBM)


def room(mib):
    return pltpu.CompilerParams(vmem_limit_bytes=mib << 20)


def call_sample(direction, halo, wind, wind_gradient, viscosity, cells, og, owners, obs):
    _, cx, cy, nz = direction.shape
    tiles = cells.shape[0]
    return pl.pallas_call(
        functools.partial(sample_kernel, obs=obs),
        name="sample",
        in_specs=[smem, hbm, vmem, vmem, vmem, vmem, hbm, hbm, hbm, vmem, vmem],
        out_specs=[vmem, vmem],
        scratch_shapes=[
            pltpu.VMEM((3, cx + 2, cy, nz), f32),
            pltpu.VMEM((3, cx, cy, nz), f32),
            pltpu.VMEM((9, cx, cy, nz), f32),
            pltpu.VMEM((cx, cy, nz), f32),
            pltpu.VMEM((3, cx * cy, 2 * nz), bf16),
            pltpu.VMEM((3, tiles, tile), f32),
            pltpu.VMEM((owners, lanes), f32),
            pltpu.VMEM((tile, tile), bf16),
            pltpu.VMEM((2 * owners, 2 * lanes), f32),
            pltpu.SemaphoreType.DMA((4, cx)),
        ],
        out_shape=[
            jax.ShapeDtypeStruct((owners // 2, 2, 4, lanes), f32),
            jax.ShapeDtypeStruct((tiles, tile), i32),
        ],
        compiler_params=room(40),
    )(cells, direction, *halo, wind, wind_gradient, viscosity, cells, og)


def call_owner(gate_counts, got, sight, precision):
    owners = got.shape[0]
    return pl.pallas_call(
        owner_kernel,
        name="owner",
        in_specs=[smem, vmem, vmem, vmem],
        out_specs=[vmem, vmem],
        scratch_shapes=[pltpu.VMEM((owners // 8, lanes, 8 * lanes), bf16)],
        out_shape=[
            jax.ShapeDtypeStruct((owners, 4, lanes), f32),
            jax.ShapeDtypeStruct((1, sight.shape[2]), f32),
        ],
        compiler_params=room(24),
    )(gate_counts, got, sight, precision)


def call_adjoint(returned, cells, slot, wind, wind_gradient, viscosity):
    _, cx, cy, nz = wind.shape
    tiles = cells.shape[0]
    half = returned.shape[0]
    return pl.pallas_call(
        adjoint_kernel,
        name="adjoint",
        in_specs=[smem, vmem, vmem, vmem, hbm, hbm, hbm],
        out_specs=[hbm, vmem, vmem, vmem, vmem],
        scratch_shapes=[
            pltpu.VMEM((3, cx, cy, nz), f32),
            pltpu.VMEM((9, cx, cy, nz), f32),
            pltpu.VMEM((cx, cy, nz), f32),
            pltpu.VMEM((3 * half, 4 * lanes), bf16),
            pltpu.VMEM((3, tiles, tile), f32),
            pltpu.VMEM((3, cx * cy, nz), f32),
            pltpu.VMEM((3, cx + 2, cy, nz), f32),
            pltpu.SemaphoreType.DMA((4, cx)),
        ],
        out_shape=[
            jax.ShapeDtypeStruct((3, cx, cy, nz), f32),
            jax.ShapeDtypeStruct((3, cy, nz), f32),
            jax.ShapeDtypeStruct((3, cy, nz), f32),
            jax.ShapeDtypeStruct((3, cx, nz), f32),
            jax.ShapeDtypeStruct((3, cx, nz), f32),
        ],
        compiler_params=room(40),
    )(cells, returned, cells, slot, wind, wind_gradient, viscosity)


def call_edges(result, halo):
    _, cx, cy, nz = result.shape
    return pl.pallas_call(
        edge_kernel,
        name="edges",
        in_specs=[hbm, vmem, vmem, vmem, vmem],
        out_specs=hbm,
        scratch_shapes=[
            pltpu.VMEM((3, cy, nz), f32),
            pltpu.VMEM((3, cy, nz), f32),
            pltpu.VMEM((3, cx - 2, 8, nz), f32),
            pltpu.VMEM((3, cx - 2, 8, nz), f32),
            pltpu.SemaphoreType.DMA((8,)),
        ],
        out_shape=jax.ShapeDtypeStruct(result.shape, f32),
        input_output_aliases={0: 0},
        compiler_params=room(24),
    )(result, *halo)


def body(
    direction,
    wind,
    wind_gradient,
    viscosity,
    sample_owner,
    sample_cell,
    sample_gate,
    sight,
    gate_counts,
    precision,
):
    _, cx, cy, nz = direction.shape
    owners = lax.axis_size("track") * lax.axis_size("cross")
    obs = sight.shape[2]
    names = ("track", "cross")
    halo = (
        shifted(direction[:, cx - 1], "track", 1),
        shifted(direction[:, 0], "track", -1),
        shifted(direction[:, :, cy - 1], "cross", 1),
        shifted(direction[:, :, 0], "cross", -1),
    )
    cells, og = lax.sort(
        (sample_cell.reshape(-1), sample_owner.reshape(-1) * obs + sample_gate.reshape(-1)), num_keys=1, is_stable=False
    )
    cells = cells.reshape(-1, tile)
    og = og.reshape(-1, tile)
    slots, slot = call_sample(direction, halo, wind, wind_gradient, viscosity, cells, og, owners, obs)
    got = lax.all_to_all(slots.reshape(owners, 4, lanes), names, split_axis=0, concat_axis=0, tiled=True)
    back, weighted = call_owner(gate_counts, got, sight, precision)
    returned = lax.all_to_all(back, names, split_axis=0, concat_axis=0, tiled=True)
    returned = returned.reshape(owners // 2, 2, 4, lanes)
    result, xlo, xhi, ylo, yhi = call_adjoint(returned, cells, slot, wind, wind_gradient, viscosity)
    result = call_edges(
        result,
        (
            shifted(xhi, "track", 1),
            shifted(xlo, "track", -1),
            shifted(yhi, "cross", 1),
            shifted(ylo, "cross", -1),
        ),
    )
    return (result, weighted)


def solution(mesh):
    placed = (
        P(None, "track", "cross", None),
        P(None, "track", "cross", None),
        P(None, "track", "cross", None),
        P("track", "cross", None),
        P("track", "cross", None, None),
        P("track", "cross", None),
        P("track", "cross", None),
        P(None, ("track", "cross"), None),
        P(("track", "cross"), None),
        P(("track", "cross"), None, None),
    )
    return jax.shard_map(
        body,
        mesh=mesh,
        in_specs=placed,
        out_specs=(P(None, "track", "cross", None), P(("track", "cross"), None)),
        check_vma=False,
    )
```

```python
import jax
import jax.numpy as jnp
from jax import lax
from jax.experimental import pallas as pl
from jax.experimental.pallas import tpu as pltpu
from jax.sharding import PartitionSpec as P

time_step = 0.2
highest = lax.Precision.HIGHEST
tile = 256
lanes = 128
span = 64
strip = 16
batch = 2
row_bits = 8
f32 = jnp.float32
bf16 = jnp.bfloat16
i32 = jnp.int32


def split(value):
    head = value.astype(bf16)
    return head, (value - head.astype(f32)).astype(bf16)


def rows_equal(count, row):
    iota = lax.broadcasted_iota(i32, (count, row.shape[1]), 0)
    return iota == row


def pick(mask, value):
    return jnp.sum(jnp.where(mask, value, 0.0), axis=0, keepdims=True)


def onehot(count, row):
    iota = lax.broadcasted_iota(i32, (count, row.shape[1]), 0).astype(bf16)
    return jnp.where(iota == row.astype(f32).astype(bf16), jnp.ones((), bf16), jnp.zeros((), bf16))


def ones_at(mask):
    return jnp.where(mask, 1.0, 0.0).astype(bf16)


def dot_nt(a, b):
    return lax.dot_general(a, b, (((1,), (1,)), ((), ())), preferred_element_type=f32)


def dot_nn(a, b):
    return jnp.dot(a, b, preferred_element_type=f32)


def window(cell_s, t, rows):
    first = cell_s[t, 0] >> row_bits
    last = cell_s[t, tile - 1] >> row_bits
    base = jnp.minimum((first >> 4) << 4, rows - span)
    return pl.multiple_of(base, 16), last - base - span + 1


def each_tile(cell_s, tiles, rows, visit, more):
    def first(t, most):
        base, over = window(cell_s, t, rows)
        visit(t, base)
        return jnp.maximum(most, over)

    most = lax.fori_loop(0, tiles, first, i32(0), unroll=16)

    @pl.when(most > 0)
    def _():
        def rest(t, carry):
            base, over = window(cell_s, t, rows)

            def step(k, carry):
                least = base + k * span
                more(t, pl.multiple_of(jnp.minimum(least, rows - span), 16), least)
                return carry

            lax.fori_loop(1, 1 + (over + span - 1) // span, step, 0)
            return carry

        lax.fori_loop(0, tiles, rest, 0)


def slot_parts(slot):
    return slot // (2 * lanes), slot % (2 * lanes)


def sample_kernel(
    cell_s,
    field_hbm,
    xlo_ref,
    xhi_ref,
    ylo_ref,
    yhi_ref,
    wind_hbm,
    grad_hbm,
    visc_hbm,
    cell_ref,
    owner_ref,
    gate_ref,
    slots_ref,
    slot_ref,
    field_ref,
    wind_ref,
    grad_ref,
    visc_ref,
    plane_ref,
    value_ref,
    offset_ref,
    upper_ref,
    total_ref,
    sems,
):
    nx, cy, nz = visc_ref.shape
    tiles = cell_ref.shape[0]
    owners = 2 * slots_ref.shape[0]
    rows = nx * cy

    def copies(k):
        part = pl.ds(k * batch, batch)
        return [
            pltpu.make_async_copy(field_hbm.at[:, part], field_ref.at[:, pl.ds(k * batch + 1, batch)], sems.at[0, k]),
            pltpu.make_async_copy(wind_hbm.at[:, part], wind_ref.at[:, part], sems.at[1, k]),
            pltpu.make_async_copy(grad_hbm.at[:, part], grad_ref.at[:, part], sems.at[2, k]),
            pltpu.make_async_copy(visc_hbm.at[part], visc_ref.at[part], sems.at[3, k]),
        ]

    batches = nx // batch
    for k in range(batches):
        for copy in copies(k):
            copy.start()

    along, across = lax.axis_index("track"), lax.axis_index("cross")
    field_ref[:, 0] = jnp.where(along == 0, 0.0, xlo_ref[...])
    field_ref[:, nx + 1] = jnp.where(along == lax.axis_size("track") - 1, 0.0, xhi_ref[...])
    left_edge = across == 0
    right_edge = across == lax.axis_size("cross") - 1

    offset_ref[...] = jnp.zeros_like(offset_ref)
    a = lax.broadcasted_iota(i32, (tile, tile), 0)
    b = lax.broadcasted_iota(i32, (tile, tile), 1)
    upper_ref[...] = ones_at(a <= b)

    def rank(t, carry):
        own = owner_ref[pl.ds(t, 1), :]
        mask = rows_equal(owners, own)
        counts = dot_nn(ones_at(mask), upper_ref[...])
        offset = offset_ref[...]
        ranks = pick(mask, counts + jnp.concatenate([offset] * (tile // lanes), axis=1))
        slot_ref[pl.ds(t, 1), :] = own * lanes + ranks.astype(i32) - 1
        offset_ref[...] = offset + jnp.broadcast_to(counts[:, tile - 1 : tile], offset.shape)
        return carry

    lax.fori_loop(0, tiles, rank, 0, unroll=16)

    y_at = lax.broadcasted_iota(i32, (strip, nz), 0)
    z_at = lax.broadcasted_iota(i32, (strip, nz), 1)

    def advance(x, carry):
        for y in range(0, cy, strip):
            part = pl.ds(y, strip)
            visc = time_step * visc_ref[x, part]
            wind = [(-0.5 * time_step) * wind_ref[a, x, part] for a in range(3)]
            here = [field_ref[c, x + 1, part] for c in range(3)]
            for c in range(3):
                f = here[c]
                down = field_ref[c, x, part]
                up = field_ref[c, x + 2, part]
                if y == 0:
                    before = jnp.where(left_edge, 0.0, ylo_ref[c, pl.ds(x, 1), :])
                else:
                    before = field_ref[c, x + 1, y - 1 : y]
                if y + strip == cy:
                    after = jnp.where(right_edge, 0.0, yhi_ref[c, pl.ds(x, 1), :])
                else:
                    after = field_ref[c, x + 1, y + strip : y + strip + 1]
                left = jnp.where(y_at == 0, before, pltpu.roll(f, 1, 0))
                right = jnp.where(y_at == strip - 1, after, pltpu.roll(f, strip - 1, 0))
                under = jnp.where(z_at == 0, 0.0, pltpu.roll(f, 1, 1))
                over = jnp.where(z_at == nz - 1, 0.0, pltpu.roll(f, nz - 1, 1))
                near = (up + down) + (right + left) + (over + under)
                tangent = f + visc * (near - 6.0 * f)
                tangent += wind[0] * (up - down) + wind[1] * (right - left) + wind[2] * (over - under)
                gq = (
                    grad_ref[3 * c, x, part] * here[0]
                    + grad_ref[3 * c + 1, x, part] * here[1]
                    + grad_ref[3 * c + 2, x, part] * here[2]
                )
                head, rest = split(tangent - time_step * gq)
                at = pl.multiple_of(x * cy + y, strip)
                plane_ref[c, pl.ds(at, strip), :nz] = head
                plane_ref[c, pl.ds(at, strip), nz:] = rest
        return carry

    copies(0)[0].wait()
    for k in range(batches):
        for copy in copies(k)[1:]:
            copy.wait()
        if k + 1 < batches:
            copies(k + 1)[0].wait()
        lax.fori_loop(k * batch, (k + 1) * batch, advance, 0)

    def find(t, begin, least):
        cells = cell_ref[pl.ds(t, 1), :]
        zs = onehot(nz, cells % nz)
        line = cells // nz
        mask = rows_equal(span, jnp.where(line >= least, line - begin, -1))
        block = jnp.concatenate(
            [plane_ref[c, pl.ds(begin, span), h * nz : (h + 1) * nz] for h in range(2) for c in range(3)], axis=0
        )
        found = dot_nn(block, zs)
        found = found[: 3 * span] + found[3 * span :]
        return [pick(mask, found[c * span : (c + 1) * span]) for c in range(3)]

    def gather(t, begin):
        for c, value in enumerate(find(t, begin, 0)):
            value_ref[c, pl.ds(t, 1), :] = value

    def gather_more(t, begin, least):
        for c, value in enumerate(find(t, begin, least)):
            value_ref[c, pl.ds(t, 1), :] += value

    each_tile(cell_s, tiles, rows, gather, gather_more)

    total_ref[...] = jnp.zeros_like(total_ref)
    half = owners // 2

    def add_tile(t, carry):
        line, column = slot_parts(slot_ref[pl.ds(t, 1), :])
        gate = gate_ref[pl.ds(t, 1), :]
        mask = rows_equal(half, line)
        columns = onehot(2 * lanes, column)
        low = gate % lanes
        parts = []
        for c in range(3):
            head, rest = split(value_ref[c, pl.ds(t, 1), :])
            parts.append((head.astype(f32), rest.astype(f32)))
        parts.append(((gate - low).astype(f32), low.astype(f32)))
        left = jnp.concatenate(
            [
                jnp.concatenate([jnp.where(mask, a, 0.0).astype(bf16), jnp.where(mask, b, 0.0).astype(bf16)], axis=1)
                for a, b in parts
            ],
            axis=0,
        )
        total_ref[...] += dot_nt(left, jnp.concatenate([columns, columns], axis=1))
        return carry

    lax.fori_loop(0, tiles, add_tile, 0, unroll=16)
    for c in range(4):
        for h in range(2):
            slots_ref[:, h, c, :] = total_ref[c * half : (c + 1) * half, h * lanes : (h + 1) * lanes]


def owner_kernel(counts_s, got_ref, sight_ref, precision_ref, back_ref, weighted_ref, gate_ref):
    sources = got_ref.shape[0]
    group = 8
    wide = group * lanes
    beams = counts_s.shape[1]

    def gathered(i):
        return jnp.concatenate([got_ref[i * group + j] for j in range(group)], axis=1)

    def beam_mask(gate):
        return rows_equal(beams, gate // lanes)

    def collect(i, acc):
        rows = gathered(i)
        gate = rows[3:4].astype(i32)
        gates = onehot(lanes, gate % lanes)
        gate_ref[i] = gates
        mask = beam_mask(gate)
        parts = []
        for k in range(3):
            head, rest = split(rows[k : k + 1])
            parts.append(jnp.where(mask, head.astype(f32), 0.0))
            parts.append(jnp.where(mask, rest.astype(f32), 0.0))
        left = jnp.concatenate(parts, axis=0).astype(bf16)
        return acc + dot_nt(left, gates)

    acc = lax.fori_loop(0, sources // group, collect, jnp.zeros((6 * beams, lanes), f32), unroll=8)
    sights = [
        jnp.concatenate([sight_ref[k, :, b * lanes : (b + 1) * lanes] for b in range(beams)], axis=0)
        for k in range(3)
    ]
    observed = jnp.zeros((beams, lanes), f32)
    for k in range(3):
        at = 2 * k * beams
        observed += sights[k] * (acc[at : at + beams] + acc[at + beams : at + 2 * beams])
    beam_at = lax.broadcasted_iota(i32, (beams, lanes), 0)
    gate_at = lax.broadcasted_iota(i32, (beams, lanes), 1)
    limit = jnp.zeros((beams, lanes), i32)
    for b in range(beams):
        limit = jnp.where(beam_at == b, counts_s[0, b], limit)
    live = jnp.where(gate_at < limit, 1.0, 0.0)
    weighted = live * jnp.dot(live * observed, precision_ref[0], precision=highest, preferred_element_type=f32)
    for b in range(beams):
        weighted_ref[:, b * lanes : (b + 1) * lanes] = weighted[b : b + 1]
    spread = jnp.concatenate([s * weighted for s in sights], axis=0)
    head = spread.astype(bf16).astype(f32)
    table = jnp.concatenate([head, spread - head], axis=0).astype(bf16)

    def give(i, carry):
        gate = gathered(i)[3:4].astype(i32)
        mask = beam_mask(gate)
        gates = gate_ref[i]
        found = dot_nn(table, gates)
        found = found[: 3 * beams] + found[3 * beams :]
        rows = jnp.concatenate(
            [pick(mask, found[k * beams : (k + 1) * beams]) for k in range(3)] + [jnp.zeros((1, wide), f32)], axis=0
        )
        for j in range(group):
            back_ref[i * group + j] = rows[:, j * lanes : (j + 1) * lanes]
        return carry

    lax.fori_loop(0, sources // group, give, 0, unroll=8)


def adjoint_kernel(
    cell_s,
    back_ref,
    cell_ref,
    slot_ref,
    wind_hbm,
    grad_hbm,
    visc_hbm,
    out_hbm,
    xlo_ref,
    xhi_ref,
    ylo_ref,
    yhi_ref,
    wind_ref,
    grad_ref,
    visc_ref,
    table_ref,
    value_ref,
    plane_ref,
    out_ref,
    sems,
):
    nx, cy, nz = visc_ref.shape
    tiles = cell_ref.shape[0]
    half = back_ref.shape[0]
    rows = nx * cy

    copies = [
        pltpu.make_async_copy(wind_hbm, wind_ref, sems.at[0, 0]),
        pltpu.make_async_copy(grad_hbm, grad_ref, sems.at[1, 0]),
        pltpu.make_async_copy(visc_hbm, visc_ref, sems.at[2, 0]),
    ]

    def write(x):
        return pltpu.make_async_copy(out_ref.at[:, x + 1], out_hbm.at[:, x], sems.at[3, x])

    for copy in copies:
        copy.start()
    for c in range(3):
        for h in range(2):
            head, rest = split(back_ref[:, h, c, :])
            table_ref[c * half : (c + 1) * half, h * lanes : (h + 1) * lanes] = head
            table_ref[(3 + c) * half : (4 + c) * half, h * lanes : (h + 1) * lanes] = rest
    plane_ref[...] = jnp.zeros_like(plane_ref)

    def restore(t, carry):
        line, column = slot_parts(slot_ref[pl.ds(t, 1), :])
        mask = rows_equal(half, line)
        columns = onehot(2 * lanes, column)
        found = dot_nn(table_ref[...], columns)
        found = found[: 3 * half] + found[3 * half :]
        for c in range(3):
            value_ref[c, pl.ds(t, 1), :] = pick(mask, found[c * half : (c + 1) * half])
        return carry

    lax.fori_loop(0, tiles, restore, 0, unroll=16)

    def put(t, begin, least):
        cells = cell_ref[pl.ds(t, 1), :]
        zs = onehot(nz, cells % nz)
        line = cells // nz
        mask = rows_equal(span, jnp.where(line >= least, line - begin, -1))
        heads, rests = [], []
        for c in range(3):
            head, rest = split(value_ref[c, pl.ds(t, 1), :])
            heads.append(jnp.where(mask, head.astype(f32), 0.0).astype(bf16))
            rests.append(jnp.where(mask, rest.astype(f32), 0.0).astype(bf16))
        added = dot_nt(jnp.concatenate(heads + rests, axis=0), zs)
        added = added[: 3 * span] + added[3 * span :]
        for c in range(3):
            plane_ref[c, pl.ds(begin, span), :] += added[c * span : (c + 1) * span]

    each_tile(cell_s, tiles, rows, lambda t, base: put(t, base, 0), put)

    y_at = lax.broadcasted_iota(i32, (strip, nz), 0)
    z_at = lax.broadcasted_iota(i32, (strip, nz), 1)
    strips = cy // strip

    def advance(x, carry):
        def give(k):
            part = pl.ds(k * strip, strip)
            at = pl.multiple_of(x * cy + k * strip, strip)
            pulled = [plane_ref[c, pl.ds(at, strip), :] for c in range(3)]
            visc = time_step * visc_ref[x, part]
            wind = (0.5 * time_step) * wind_ref[1, x, part]
            mixed = [visc * p for p in pulled]
            moved = [wind * p for p in pulled]
            return pulled, mixed, [m + w for m, w in zip(mixed, moved)], [m - w for m, w in zip(mixed, moved)]

        later = give(0)
        before = [0.0] * 3
        for k in range(strips):
            pulled, mixed, to_left, to_right = later
            part = pl.ds(k * strip, strip)
            after = [0.0] * 3
            if k + 1 < strips:
                later = give(k + 1)
                after = [v[0:1] for v in later[2]]
            wind_x = (0.5 * time_step) * wind_ref[0, x, part]
            wind_z = (0.5 * time_step) * wind_ref[2, x, part]
            for c in range(3):
                p = pulled[c]
                sx = wind_x * p
                sz = wind_z * p
                gtr = (
                    grad_ref[c, x, part] * pulled[0]
                    + grad_ref[3 + c, x, part] * pulled[1]
                    + grad_ref[6 + c, x, part] * pulled[2]
                )
                around = (
                    jnp.where(y_at == strip - 1, after[c], pltpu.roll(to_left[c], strip - 1, 0))
                    + jnp.where(y_at == 0, before[c], pltpu.roll(to_right[c], 1, 0))
                ) + (
                    jnp.where(z_at == nz - 1, 0.0, pltpu.roll(mixed[c] + sz, nz - 1, 1))
                    + jnp.where(z_at == 0, 0.0, pltpu.roll(mixed[c] - sz, 1, 1))
                )
                own = (p - 6.0 * mixed[c]) + (around - time_step * gtr)
                out_ref[c, x, part] += mixed[c] + sx
                out_ref[c, x + 1, part] += own
                out_ref[c, x + 2, part] = mixed[c] - sx
            if k == 0:
                for c in range(3):
                    ylo_ref[c, pl.ds(x, 1), :] = to_left[c][0:1]
            if k + 1 == strips:
                for c in range(3):
                    yhi_ref[c, pl.ds(x, 1), :] = to_right[c][strip - 1 : strip]
            before = [v[strip - 1 : strip] for v in to_right]

        @pl.when(x > 0)
        def _():
            write(x - 1).start()

        return carry

    for copy in copies:
        copy.wait()
    out_ref[:, 0:2] = jnp.zeros((3, 2, cy, nz), f32)
    lax.fori_loop(0, nx, advance, 0)
    xlo_ref[...] = out_ref[:, 0]
    xhi_ref[...] = out_ref[:, nx + 1]
    write(nx - 1).start()

    def end(x, carry):
        write(x).wait()
        return carry

    lax.fori_loop(0, nx, end, 0)


def edge_kernel(
    given_ref, xlo_ref, xhi_ref, ylo_ref, yhi_ref, out_ref, low_ref, high_ref, left_ref, right_ref, sems
):
    del given_ref
    along, across = lax.axis_index("track"), lax.axis_index("cross")
    last_along, last_across = lax.axis_size("track") - 1, lax.axis_size("cross") - 1
    ylo = jnp.where(across == 0, 0.0, ylo_ref[...])
    yhi = jnp.where(across == last_across, 0.0, yhi_ref[...])
    nx, cy = out_ref.shape[1], out_ref.shape[2]
    inner = nx - 2
    places = [
        (out_ref.at[:, 0], low_ref),
        (out_ref.at[:, nx - 1], high_ref),
        (out_ref.at[:, pl.ds(1, inner), pl.ds(0, 8)], left_ref),
        (out_ref.at[:, pl.ds(1, inner), pl.ds(cy - 8, 8)], right_ref),
    ]
    reads = [pltpu.make_async_copy(a, b, sems.at[i]) for i, (a, b) in enumerate(places)]
    for read in reads:
        read.start()
    writes = [pltpu.make_async_copy(b, a, sems.at[4 + i]) for i, (a, b) in enumerate(places)]
    for i, (x, ref, halo, edge) in enumerate(
        ((0, low_ref, xlo_ref, along == 0), (nx - 1, high_ref, xhi_ref, along == last_along))
    ):
        reads[i].wait()
        ref[...] += jnp.where(edge, 0.0, halo[...])
        ref[:, 0:1, :] += ylo[:, x : x + 1, :]
        ref[:, cy - 1 : cy, :] += yhi[:, x : x + 1, :]
        writes[i].start()
    reads[2].wait()
    for k in range(inner):
        left_ref[:, k, 0:1, :] += ylo[:, k + 1 : k + 2, :]
    writes[2].start()
    reads[3].wait()
    for k in range(inner):
        right_ref[:, k, 7:8, :] += yhi[:, k + 1 : k + 2, :]
    writes[3].start()
    for write in writes:
        write.wait()


def shifted(value, axis, by):
    count = lax.axis_size(axis)
    return lax.ppermute(value, axis, [(i, (i + by) % count) for i in range(count)])


vmem = pl.BlockSpec(memory_space=pltpu.VMEM)
smem = pl.BlockSpec(memory_space=pltpu.SMEM)
hbm = pl.BlockSpec(memory_space=pltpu.HBM)


def held(value):
    return pltpu.with_memory_space_constraint(value, pltpu.HBM)


def room(mib):
    return pltpu.CompilerParams(vmem_limit_bytes=mib << 20)


def call_sample(direction, halo, wind, wind_gradient, viscosity, cells, owner, gate, owners):
    _, cx, cy, nz = direction.shape
    tiles = cells.shape[0]
    return pl.pallas_call(
        sample_kernel,
        name="sample",
        in_specs=[smem, hbm, vmem, vmem, vmem, vmem, hbm, hbm, hbm, vmem, vmem, vmem],
        out_specs=[vmem, vmem],
        scratch_shapes=[
            pltpu.VMEM((3, cx + 2, cy, nz), f32),
            pltpu.VMEM((3, cx, cy, nz), f32),
            pltpu.VMEM((9, cx, cy, nz), f32),
            pltpu.VMEM((cx, cy, nz), f32),
            pltpu.VMEM((3, cx * cy, 2 * nz), bf16),
            pltpu.VMEM((3, tiles, tile), f32),
            pltpu.VMEM((owners, lanes), f32),
            pltpu.VMEM((tile, tile), bf16),
            pltpu.VMEM((2 * owners, 2 * lanes), f32),
            pltpu.SemaphoreType.DMA((4, cx)),
        ],
        out_shape=[
            jax.ShapeDtypeStruct((owners // 2, 2, 4, lanes), f32),
            jax.ShapeDtypeStruct((tiles, tile), i32),
        ],
        compiler_params=room(40),
    )(cells, held(direction), *halo, held(wind), held(wind_gradient), held(viscosity), cells, owner, gate)


def call_owner(gate_counts, got, sight, precision):
    owners = got.shape[0]
    return pl.pallas_call(
        owner_kernel,
        name="owner",
        in_specs=[smem, vmem, vmem, vmem],
        out_specs=[vmem, vmem],
        scratch_shapes=[pltpu.VMEM((owners // 8, lanes, 8 * lanes), bf16)],
        out_shape=[
            jax.ShapeDtypeStruct((owners, 4, lanes), f32),
            jax.ShapeDtypeStruct((1, sight.shape[2]), f32),
        ],
        compiler_params=room(24),
    )(gate_counts, got, sight, precision)


def call_adjoint(returned, cells, slot, wind, wind_gradient, viscosity):
    _, cx, cy, nz = wind.shape
    tiles = cells.shape[0]
    half = returned.shape[0]
    return pl.pallas_call(
        adjoint_kernel,
        name="adjoint",
        in_specs=[smem, vmem, vmem, vmem, hbm, hbm, hbm],
        out_specs=[hbm, vmem, vmem, vmem, vmem],
        scratch_shapes=[
            pltpu.VMEM((3, cx, cy, nz), f32),
            pltpu.VMEM((9, cx, cy, nz), f32),
            pltpu.VMEM((cx, cy, nz), f32),
            pltpu.VMEM((6 * half, 2 * lanes), bf16),
            pltpu.VMEM((3, tiles, tile), f32),
            pltpu.VMEM((3, cx * cy, nz), f32),
            pltpu.VMEM((3, cx + 2, cy, nz), f32),
            pltpu.SemaphoreType.DMA((4, cx)),
        ],
        out_shape=[
            jax.ShapeDtypeStruct((3, cx, cy, nz), f32),
            jax.ShapeDtypeStruct((3, cy, nz), f32),
            jax.ShapeDtypeStruct((3, cy, nz), f32),
            jax.ShapeDtypeStruct((3, cx, nz), f32),
            jax.ShapeDtypeStruct((3, cx, nz), f32),
        ],
        compiler_params=room(40),
    )(cells, returned, cells, slot, held(wind), held(wind_gradient), held(viscosity))


def call_edges(result, halo):
    _, cx, cy, nz = result.shape
    return pl.pallas_call(
        edge_kernel,
        name="edges",
        in_specs=[hbm, vmem, vmem, vmem, vmem],
        out_specs=hbm,
        scratch_shapes=[
            pltpu.VMEM((3, cy, nz), f32),
            pltpu.VMEM((3, cy, nz), f32),
            pltpu.VMEM((3, cx - 2, 8, nz), f32),
            pltpu.VMEM((3, cx - 2, 8, nz), f32),
            pltpu.SemaphoreType.DMA((8,)),
        ],
        out_shape=jax.ShapeDtypeStruct(result.shape, f32),
        input_output_aliases={0: 0},
        compiler_params=room(24),
    )(result, *halo)


def body(
    direction,
    wind,
    wind_gradient,
    viscosity,
    sample_owner,
    sample_cell,
    sample_gate,
    sight,
    gate_counts,
    precision,
):
    _, cx, cy, nz = direction.shape
    owners = lax.axis_size("track") * lax.axis_size("cross")
    names = ("track", "cross")
    halo = (
        shifted(direction[:, cx - 1], "track", 1),
        shifted(direction[:, 0], "track", -1),
        shifted(direction[:, :, cy - 1], "cross", 1),
        shifted(direction[:, :, 0], "cross", -1),
    )
    cells, owner, gate = [
        v.reshape(-1, tile)
        for v in lax.sort(
            (sample_cell.reshape(-1), sample_owner.reshape(-1), sample_gate.reshape(-1)), num_keys=1, is_stable=False
        )
    ]
    slots, slot = call_sample(direction, halo, wind, wind_gradient, viscosity, cells, owner, gate, owners)
    got = lax.all_to_all(slots.reshape(owners, 4, lanes), names, split_axis=0, concat_axis=0, tiled=True)
    back, weighted = call_owner(gate_counts, got, sight, precision)
    returned = lax.all_to_all(back, names, split_axis=0, concat_axis=0, tiled=True)
    returned = returned.reshape(owners // 2, 2, 4, lanes)
    result, xlo, xhi, ylo, yhi = call_adjoint(returned, cells, slot, wind, wind_gradient, viscosity)
    result = call_edges(
        result,
        (
            shifted(xhi, "track", 1),
            shifted(xlo, "track", -1),
            shifted(yhi, "cross", 1),
            shifted(ylo, "cross", -1),
        ),
    )
    return (result, weighted)


def solution(mesh):
    placed = (
        P(None, "track", "cross", None),
        P(None, "track", "cross", None),
        P(None, "track", "cross", None),
        P("track", "cross", None),
        P("track", "cross", None, None),
        P("track", "cross", None),
        P("track", "cross", None),
        P(None, ("track", "cross"), None),
        P(("track", "cross"), None),
        P(("track", "cross"), None, None),
    )
    return jax.shard_map(
        body,
        mesh=mesh,
        in_specs=placed,
        out_specs=(P(None, "track", "cross", None), P(("track", "cross"), None)),
        check_vma=False,
    )
```

```python
import jax
import jax.numpy as jnp
from jax import lax
from jax.experimental import pallas as pl
from jax.experimental.pallas import tpu as pltpu
from jax.sharding import PartitionSpec as P

time_step = 0.2
highest = lax.Precision.HIGHEST
tile = 256
lanes = 128
span = 64
strip = 16
batch = 2
row_bits = 8
f32 = jnp.float32
bf16 = jnp.bfloat16
i32 = jnp.int32


def split(value):
    head = value.astype(bf16)
    return head, (value - head.astype(f32)).astype(bf16)


def rows_equal(count, row):
    iota = lax.broadcasted_iota(i32, (count, row.shape[1]), 0)
    return iota == row


def pick(mask, value):
    return jnp.sum(jnp.where(mask, value, 0.0), axis=0, keepdims=True)


def onehot(count, row):
    iota = lax.broadcasted_iota(i32, (count, row.shape[1]), 0).astype(bf16)
    return jnp.where(iota == row.astype(f32).astype(bf16), jnp.ones((), bf16), jnp.zeros((), bf16))


def ones_at(mask):
    return jnp.where(mask, 1.0, 0.0).astype(bf16)


def dot_nt(a, b):
    return lax.dot_general(a, b, (((1,), (1,)), ((), ())), preferred_element_type=f32)


def dot_nn(a, b):
    return jnp.dot(a, b, preferred_element_type=f32)


def shift_rows(value, edge, by):
    count, wide = value.shape
    row = lax.broadcasted_iota(i32, (8, wide), 0)
    parts = [value[k : k + 8] for k in range(0, count, 8)]
    turned = [pltpu.roll(p, by % 8, 0) for p in parts]
    if by > 0:
        inner, beside = row == 0, [jnp.broadcast_to(edge, (8, wide))] + turned[:-1]
    else:
        inner, beside = row == 7, turned[1:] + [jnp.broadcast_to(edge, (8, wide))]
    return jnp.concatenate([jnp.where(inner, b, a) for a, b in zip(turned, beside)], axis=0)


def window(cell_s, t, rows):
    first = cell_s[t, 0] >> row_bits
    last = cell_s[t, tile - 1] >> row_bits
    base = jnp.minimum((first >> 4) << 4, rows - span)
    return pl.multiple_of(base, 16), last - base - span + 1


def each_tile(cell_s, tiles, rows, visit, more):
    def first(t, most):
        base, over = window(cell_s, t, rows)
        visit(t, base)
        return jnp.maximum(most, over)

    most = lax.fori_loop(0, tiles, first, i32(0), unroll=16)

    @pl.when(most > 0)
    def _():
        def rest(t, carry):
            base, over = window(cell_s, t, rows)

            def step(k, carry):
                least = base + k * span
                more(t, pl.multiple_of(jnp.minimum(least, rows - span), 16), least)
                return carry

            lax.fori_loop(1, 1 + (over + span - 1) // span, step, 0)
            return carry

        lax.fori_loop(0, tiles, rest, 0)


def slot_parts(slot):
    return slot // (2 * lanes), slot % (2 * lanes)


def border_kernel(field_hbm, xlo_ref, xhi_ref, ylo_ref, yhi_ref, low_ref, high_ref, sems):
    nx, cy = field_hbm.shape[1], field_hbm.shape[2]
    copies = [
        pltpu.make_async_copy(field_hbm.at[:, :, pl.ds(0, 8)], low_ref, sems.at[0]),
        pltpu.make_async_copy(field_hbm.at[:, :, pl.ds(cy - 8, 8)], high_ref, sems.at[1]),
        pltpu.make_async_copy(field_hbm.at[:, 0], xlo_ref, sems.at[2]),
        pltpu.make_async_copy(field_hbm.at[:, nx - 1], xhi_ref, sems.at[3]),
    ]
    for copy in copies:
        copy.start()
    for copy, ref, into, at in ((copies[0], low_ref, ylo_ref, 0), (copies[1], high_ref, yhi_ref, 7)):
        copy.wait()
        for c in range(3):
            for x in range(nx):
                into[c, x : x + 1] = ref[c, x, at : at + 1]
    copies[2].wait()
    copies[3].wait()


def sample_kernel(
    field_hbm,
    xlo_ref,
    xhi_ref,
    ylo_ref,
    yhi_ref,
    wind_hbm,
    grad_hbm,
    visc_hbm,
    cell_ref,
    owner_ref,
    gate_ref,
    slots_ref,
    slot_ref,
    field_ref,
    wind_ref,
    grad_ref,
    visc_ref,
    plane_ref,
    value_ref,
    offset_ref,
    upper_ref,
    total_ref,
    cell_s,
    sems,
    cell_sem,
):
    nx, cy, nz = visc_ref.shape
    tiles = cell_ref.shape[0]
    owners = 2 * slots_ref.shape[0]
    rows = nx * cy

    def copies(k):
        part = pl.ds(k * batch, batch)
        return [
            pltpu.make_async_copy(field_hbm.at[:, part], field_ref.at[:, pl.ds(k * batch + 1, batch)], sems.at[0, k]),
            pltpu.make_async_copy(wind_hbm.at[:, part], wind_ref.at[:, part], sems.at[1, k]),
            pltpu.make_async_copy(grad_hbm.at[:, part], grad_ref.at[:, part], sems.at[2, k]),
            pltpu.make_async_copy(visc_hbm.at[part], visc_ref.at[part], sems.at[3, k]),
        ]

    list_cells = pltpu.make_async_copy(cell_ref, cell_s, cell_sem)
    list_cells.start()
    batches = nx // batch
    for k in range(batches):
        for copy in copies(k):
            copy.start()

    along, across = lax.axis_index("track"), lax.axis_index("cross")
    field_ref[:, 0] = jnp.where(along == 0, 0.0, xlo_ref[...])
    field_ref[:, nx + 1] = jnp.where(along == lax.axis_size("track") - 1, 0.0, xhi_ref[...])
    left_edge = across == 0
    right_edge = across == lax.axis_size("cross") - 1

    offset_ref[...] = jnp.zeros_like(offset_ref)
    a = lax.broadcasted_iota(i32, (tile, tile), 0)
    b = lax.broadcasted_iota(i32, (tile, tile), 1)
    upper_ref[...] = ones_at(a <= b)

    def rank(t, carry):
        own = owner_ref[pl.ds(t, 1), :]
        mask = rows_equal(owners, own)
        counts = dot_nn(ones_at(mask), upper_ref[...])
        offset = offset_ref[...]
        ranks = pick(mask, counts + jnp.concatenate([offset] * (tile // lanes), axis=1))
        slot_ref[pl.ds(t, 1), :] = own * lanes + ranks.astype(i32) - 1
        offset_ref[...] = offset + jnp.broadcast_to(counts[:, tile - 1 : tile], offset.shape)
        return carry

    lax.fori_loop(0, tiles, rank, 0, unroll=16)

    z_at = lax.broadcasted_iota(i32, (strip, nz), 1)

    def advance(x, carry):
        for y in range(0, cy, strip):
            part = pl.ds(y, strip)
            visc = time_step * visc_ref[x, part]
            wind = [(0.5 * time_step) * wind_ref[a, x, part] for a in range(3)]
            from_up, from_right, from_over = [visc - w for w in wind]
            from_down, from_left, from_under = [visc + w for w in wind]
            from_over = jnp.where(z_at == nz - 1, 0.0, from_over)
            from_under = jnp.where(z_at == 0, 0.0, from_under)
            own = 1.0 - 6.0 * visc
            here = [field_ref[c, x + 1, part] for c in range(3)]
            scaled = [time_step * f for f in here]
            for c in range(3):
                f = here[c]
                if y == 0:
                    before = jnp.where(left_edge, 0.0, ylo_ref[c, pl.ds(x, 1), :])
                else:
                    before = field_ref[c, x + 1, y - 1 : y]
                if y + strip == cy:
                    after = jnp.where(right_edge, 0.0, yhi_ref[c, pl.ds(x, 1), :])
                else:
                    after = field_ref[c, x + 1, y + strip : y + strip + 1]
                tangent = (
                    (own * f + from_up * field_ref[c, x + 2, part])
                    + (from_down * field_ref[c, x, part] + from_left * shift_rows(f, before, 1))
                    + (from_right * shift_rows(f, after, -1) + from_under * pltpu.roll(f, 1, 1))
                    + from_over * pltpu.roll(f, nz - 1, 1)
                ) - (
                    grad_ref[3 * c, x, part] * scaled[0]
                    + grad_ref[3 * c + 1, x, part] * scaled[1]
                    + grad_ref[3 * c + 2, x, part] * scaled[2]
                )
                head, rest = split(tangent)
                at = pl.multiple_of(x * cy + y, strip)
                plane_ref[c, pl.ds(at, strip), :nz] = head
                plane_ref[c, pl.ds(at, strip), nz:] = rest
        return carry

    copies(0)[0].wait()
    for k in range(batches):
        for copy in copies(k)[1:]:
            copy.wait()
        if k + 1 < batches:
            copies(k + 1)[0].wait()
        lax.fori_loop(k * batch, (k + 1) * batch, advance, 0)

    list_cells.wait()

    def find(t, begin, least):
        cells = cell_ref[pl.ds(t, 1), :]
        zs = onehot(nz, cells % nz)
        line = cells // nz
        mask = rows_equal(span, jnp.where(line >= least, line - begin, -1))
        block = jnp.concatenate(
            [plane_ref[c, pl.ds(begin, span), h * nz : (h + 1) * nz] for h in range(2) for c in range(3)], axis=0
        )
        found = dot_nn(block, zs)
        found = found[: 3 * span] + found[3 * span :]
        return [pick(mask, found[c * span : (c + 1) * span]) for c in range(3)]

    def gather(t, begin):
        for c, value in enumerate(find(t, begin, 0)):
            value_ref[c, pl.ds(t, 1), :] = value

    def gather_more(t, begin, least):
        for c, value in enumerate(find(t, begin, least)):
            value_ref[c, pl.ds(t, 1), :] += value

    each_tile(cell_s, tiles, rows, gather, gather_more)

    total_ref[...] = jnp.zeros_like(total_ref)
    half = owners // 2

    def add_tile(t, carry):
        line, column = slot_parts(slot_ref[pl.ds(t, 1), :])
        gate = gate_ref[pl.ds(t, 1), :]
        mask = rows_equal(half, line)
        columns = onehot(2 * lanes, column)
        low = gate % lanes
        parts = []
        for c in range(3):
            head, rest = split(value_ref[c, pl.ds(t, 1), :])
            parts.append((head.astype(f32), rest.astype(f32)))
        parts.append(((gate - low).astype(f32), low.astype(f32)))
        left = jnp.concatenate(
            [
                jnp.concatenate([jnp.where(mask, a, 0.0).astype(bf16), jnp.where(mask, b, 0.0).astype(bf16)], axis=1)
                for a, b in parts
            ],
            axis=0,
        )
        total_ref[...] += dot_nt(left, jnp.concatenate([columns, columns], axis=1))
        return carry

    lax.fori_loop(0, tiles, add_tile, 0, unroll=16)
    for c in range(4):
        for h in range(2):
            slots_ref[:, h, c, :] = total_ref[c * half : (c + 1) * half, h * lanes : (h + 1) * lanes]


def owner_kernel(counts_s, got_ref, sight_ref, precision_ref, back_ref, weighted_ref, gate_ref):
    sources = got_ref.shape[0]
    group = 8
    wide = group * lanes
    beams = counts_s.shape[1]

    def gathered(i):
        return jnp.concatenate([got_ref[i * group + j] for j in range(group)], axis=1)

    def beam_mask(gate):
        return rows_equal(beams, gate // lanes)

    def collect(i, acc):
        rows = gathered(i)
        gate = rows[3:4].astype(i32)
        gates = onehot(lanes, gate % lanes)
        gate_ref[i] = gates
        mask = beam_mask(gate)
        parts = []
        for k in range(3):
            head, rest = split(rows[k : k + 1])
            parts.append(jnp.where(mask, head.astype(f32), 0.0))
            parts.append(jnp.where(mask, rest.astype(f32), 0.0))
        left = jnp.concatenate(parts, axis=0).astype(bf16)
        return acc + dot_nt(left, gates)

    acc = lax.fori_loop(0, sources // group, collect, jnp.zeros((6 * beams, lanes), f32), unroll=8)
    sights = [
        jnp.concatenate([sight_ref[k, :, b * lanes : (b + 1) * lanes] for b in range(beams)], axis=0)
        for k in range(3)
    ]
    observed = jnp.zeros((beams, lanes), f32)
    for k in range(3):
        at = 2 * k * beams
        observed += sights[k] * (acc[at : at + beams] + acc[at + beams : at + 2 * beams])
    beam_at = lax.broadcasted_iota(i32, (beams, lanes), 0)
    gate_at = lax.broadcasted_iota(i32, (beams, lanes), 1)
    limit = jnp.zeros((beams, lanes), i32)
    for b in range(beams):
        limit = jnp.where(beam_at == b, counts_s[0, b], limit)
    live = jnp.where(gate_at < limit, 1.0, 0.0)
    weighted = live * jnp.dot(live * observed, precision_ref[0], precision=highest, preferred_element_type=f32)
    for b in range(beams):
        weighted_ref[:, b * lanes : (b + 1) * lanes] = weighted[b : b + 1]
    spread = jnp.concatenate([s * weighted for s in sights], axis=0)
    head = spread.astype(bf16).astype(f32)
    table = jnp.concatenate([head, spread - head], axis=0).astype(bf16)

    def give(i, carry):
        gate = gathered(i)[3:4].astype(i32)
        mask = beam_mask(gate)
        gates = gate_ref[i]
        found = dot_nn(table, gates)
        found = found[: 3 * beams] + found[3 * beams :]
        rows = jnp.concatenate(
            [pick(mask, found[k * beams : (k + 1) * beams]) for k in range(3)] + [jnp.zeros((1, wide), f32)], axis=0
        )
        for j in range(group):
            back_ref[i * group + j] = rows[:, j * lanes : (j + 1) * lanes]
        return carry

    lax.fori_loop(0, sources // group, give, 0, unroll=8)


def scatter_kernel(
    back_ref,
    cell_ref,
    slot_ref,
    wind_hbm,
    grad_hbm,
    visc_hbm,
    plane_ref,
    wind_ref,
    grad_ref,
    visc_ref,
    xlo_ref,
    xhi_ref,
    ylo_ref,
    yhi_ref,
    table_ref,
    value_ref,
    cell_s,
    sems,
    cell_sem,
):
    nx, cy, nz = visc_hbm.shape
    tiles = cell_ref.shape[0]
    half = back_ref.shape[0]
    rows = nx * cy
    list_cells = pltpu.make_async_copy(cell_ref, cell_s, cell_sem)
    list_cells.start()
    copies = [
        pltpu.make_async_copy(visc_hbm, visc_ref, sems.at[0]),
        pltpu.make_async_copy(wind_hbm, wind_ref, sems.at[1]),
        pltpu.make_async_copy(grad_hbm, grad_ref, sems.at[2]),
    ]
    for copy in copies:
        copy.start()
    for c in range(3):
        for h in range(2):
            head, rest = split(back_ref[:, h, c, :])
            table_ref[c * half : (c + 1) * half, h * lanes : (h + 1) * lanes] = head
            table_ref[(3 + c) * half : (4 + c) * half, h * lanes : (h + 1) * lanes] = rest
    plane_ref[...] = jnp.zeros_like(plane_ref)

    def restore(t, carry):
        line, column = slot_parts(slot_ref[pl.ds(t, 1), :])
        mask = rows_equal(half, line)
        columns = onehot(2 * lanes, column)
        found = dot_nn(table_ref[...], columns)
        found = found[: 3 * half] + found[3 * half :]
        for c in range(3):
            value_ref[c, pl.ds(t, 1), :] = pick(mask, found[c * half : (c + 1) * half])
        return carry

    lax.fori_loop(0, tiles, restore, 0, unroll=16)

    list_cells.wait()

    def put(t, begin, least):
        cells = cell_ref[pl.ds(t, 1), :]
        zs = onehot(nz, cells % nz)
        line = cells // nz
        mask = rows_equal(span, jnp.where(line >= least, line - begin, -1))
        heads, rests = [], []
        for c in range(3):
            head, rest = split(value_ref[c, pl.ds(t, 1), :])
            heads.append(jnp.where(mask, head.astype(f32), 0.0).astype(bf16))
            rests.append(jnp.where(mask, rest.astype(f32), 0.0).astype(bf16))
        added = dot_nt(jnp.concatenate(heads + rests, axis=0), zs)
        added = added[: 3 * span] + added[3 * span :]
        for c in range(3):
            plane_ref[c, pl.ds(begin, span), :] += added[c * span : (c + 1) * span]

    each_tile(cell_s, tiles, rows, lambda t, base: put(t, base, 0), put)

    for copy in copies:
        copy.wait()
    for x, ref, sign in ((0, xlo_ref, 1.0), (nx - 1, xhi_ref, -1.0)):
        passed = time_step * visc_ref[x] + (sign * 0.5 * time_step) * wind_ref[0, x]
        for c in range(3):
            ref[c] = passed * plane_ref[c, x * cy : (x + 1) * cy]
    for y, ref, sign in ((0, ylo_ref, 1.0), (cy - 1, yhi_ref, -1.0)):
        for x in range(nx):
            row = slice(y, y + 1)
            passed = time_step * visc_ref[x, row] + (sign * 0.5 * time_step) * wind_ref[1, x, row]
            for c in range(3):
                ref[c, x : x + 1] = passed * plane_ref[c, x * cy + y : x * cy + y + 1]


def adjoint_kernel(
    plane_ref, wind_ref, grad_ref, visc_ref, out_hbm, low_ref, high_ref, left_ref, right_ref, out_ref, sems
):
    nx, cy, nz = visc_ref.shape

    def write(x):
        return pltpu.make_async_copy(out_ref.at[:, x + 1], out_hbm.at[:, x], sems.at[x])

    z_at = lax.broadcasted_iota(i32, (strip, nz), 1)
    strips = cy // strip

    def advance(x, carry):
        def give(k):
            part = pl.ds(k * strip, strip)
            at = pl.multiple_of(x * cy + k * strip, strip)
            pulled = [plane_ref[c, pl.ds(at, strip), :] for c in range(3)]
            visc = time_step * visc_ref[x, part]
            wind = (0.5 * time_step) * wind_ref[1, x, part]
            to_left, to_right = visc + wind, visc - wind
            return pulled, visc, [to_left * p for p in pulled], [to_right * p for p in pulled]

        later = give(0)
        before = [jnp.zeros((1, nz), f32)] * 3
        for k in range(strips):
            pulled, visc, to_left, to_right = later
            part = pl.ds(k * strip, strip)
            after = [jnp.zeros((1, nz), f32)] * 3
            if k + 1 < strips:
                later = give(k + 1)
                after = [v[0:1] for v in later[2]]
            wind_x = (0.5 * time_step) * wind_ref[0, x, part]
            wind_z = (0.5 * time_step) * wind_ref[2, x, part]
            to_down, to_up = visc + wind_x, visc - wind_x
            to_under = jnp.where(z_at == 0, 0.0, visc + wind_z)
            to_over = jnp.where(z_at == nz - 1, 0.0, visc - wind_z)
            own = 1.0 - 6.0 * visc
            scaled = [time_step * p for p in pulled]
            for c in range(3):
                p = pulled[c]
                around = (shift_rows(to_left[c], after[c], -1) + shift_rows(to_right[c], before[c], 1)) + (
                    pltpu.roll(to_under * p, nz - 1, 1) + pltpu.roll(to_over * p, 1, 1)
                )
                gtr = (
                    grad_ref[c, x, part] * scaled[0]
                    + grad_ref[3 + c, x, part] * scaled[1]
                    + grad_ref[6 + c, x, part] * scaled[2]
                )
                out_ref[c, x, part] += to_down * p
                out_ref[c, x + 1, part] += own * p + (around - gtr)
                out_ref[c, x + 2, part] = to_up * p
            before = [v[strip - 1 : strip] for v in to_right]

        @pl.when(x > 0)
        def _():
            write(x - 1).start()

        return carry

    out_ref[:, 0:2] = jnp.zeros((3, 2, cy, nz), f32)
    lax.fori_loop(0, nx, advance, 0)
    low_ref[...] = out_ref[:, 1]
    high_ref[...] = out_ref[:, nx]
    left_ref[...] = out_ref[:, 2:nx, 0:8]
    right_ref[...] = out_ref[:, 2:nx, cy - 8 : cy]
    write(nx - 1).start()

    def end(x, carry):
        write(x).wait()
        return carry

    lax.fori_loop(0, nx, end, 0)


def edge_kernel(
    given_ref, low_ref, high_ref, left_ref, right_ref, xlo_ref, xhi_ref, ylo_ref, yhi_ref, out_ref, *scratch
):
    del given_ref
    *held_refs, sems = scratch
    along, across = lax.axis_index("track"), lax.axis_index("cross")
    last_along, last_across = lax.axis_size("track") - 1, lax.axis_size("cross") - 1
    nx, cy = out_ref.shape[1], out_ref.shape[2]
    inner = nx - 2
    left_edge, right_edge = across == 0, across == last_across
    places = [
        out_ref.at[:, 0],
        out_ref.at[:, nx - 1],
        out_ref.at[:, pl.ds(1, inner), pl.ds(0, 8)],
        out_ref.at[:, pl.ds(1, inner), pl.ds(cy - 8, 8)],
    ]
    writes = [pltpu.make_async_copy(a, b, sems.at[i]) for i, (a, b) in enumerate(zip(held_refs, places))]
    sides = (
        (0, held_refs[0], low_ref, xlo_ref, along == 0),
        (nx - 1, held_refs[1], high_ref, xhi_ref, along == last_along),
    )
    for i, (x, ref, own, halo, edge) in enumerate(sides):
        for c in range(3):
            ref[c] = own[c] + jnp.where(edge, 0.0, halo[c])
            ref[c, 0:1] += jnp.where(left_edge, 0.0, ylo_ref[c, x : x + 1])
            ref[c, cy - 1 : cy] += jnp.where(right_edge, 0.0, yhi_ref[c, x : x + 1])
        writes[i].start()
    row_at = lax.broadcasted_iota(i32, (8, out_ref.shape[3]), 0)
    for i, row, own, halo, edge in ((2, 0, left_ref, ylo_ref, left_edge), (3, 7, right_ref, yhi_ref, right_edge)):
        ref = held_refs[i]
        here = (row_at == row) & jnp.logical_not(edge)
        for c in range(3):
            for k in range(inner):
                ref[c, k] = own[c, k] + jnp.where(here, halo[c, k + 1 : k + 2], 0.0)
        writes[i].start()
    for write in writes:
        write.wait()


def shifted(value, axis, by):
    count = lax.axis_size(axis)
    return lax.ppermute(value, axis, [(i, (i + by) % count) for i in range(count)])


vmem = pl.BlockSpec(memory_space=pltpu.VMEM)
smem = pl.BlockSpec(memory_space=pltpu.SMEM)
hbm = pl.BlockSpec(memory_space=pltpu.HBM)


def held(value):
    return pltpu.with_memory_space_constraint(value, pltpu.HBM)


def room(mib):
    return pltpu.CompilerParams(vmem_limit_bytes=mib << 20)


def call_border(field):
    _, cx, cy, nz = field.shape
    return pl.pallas_call(
        border_kernel,
        name="border",
        in_specs=[hbm],
        out_specs=[vmem] * 4,
        scratch_shapes=[
            pltpu.VMEM((3, cx, 8, nz), f32),
            pltpu.VMEM((3, cx, 8, nz), f32),
            pltpu.SemaphoreType.DMA((4,)),
        ],
        out_shape=[
            jax.ShapeDtypeStruct((3, cy, nz), f32),
            jax.ShapeDtypeStruct((3, cy, nz), f32),
            jax.ShapeDtypeStruct((3, cx, nz), f32),
            jax.ShapeDtypeStruct((3, cx, nz), f32),
        ],
        compiler_params=room(8),
    )(held(field))


def call_sample(direction, halo, wind, wind_gradient, viscosity, cells, owner, gate, owners):
    _, cx, cy, nz = direction.shape
    tiles = cells.shape[0]
    return pl.pallas_call(
        sample_kernel,
        name="sample",
        in_specs=[hbm, vmem, vmem, vmem, vmem, hbm, hbm, hbm, vmem, vmem, vmem],
        out_specs=[vmem, vmem],
        scratch_shapes=[
            pltpu.VMEM((3, cx + 2, cy, nz), f32),
            pltpu.VMEM((3, cx, cy, nz), f32),
            pltpu.VMEM((9, cx, cy, nz), f32),
            pltpu.VMEM((cx, cy, nz), f32),
            pltpu.VMEM((3, cx * cy, 2 * nz), bf16),
            pltpu.VMEM((3, tiles, tile), f32),
            pltpu.VMEM((owners, lanes), f32),
            pltpu.VMEM((tile, tile), bf16),
            pltpu.VMEM((2 * owners, 2 * lanes), f32),
            pltpu.SMEM((tiles, tile), i32),
            pltpu.SemaphoreType.DMA((4, cx)),
            pltpu.SemaphoreType.DMA,
        ],
        out_shape=[
            jax.ShapeDtypeStruct((owners // 2, 2, 4, lanes), f32),
            jax.ShapeDtypeStruct((tiles, tile), i32),
        ],
        compiler_params=room(40),
    )(held(direction), *halo, held(wind), held(wind_gradient), held(viscosity), cells, owner, gate)


def call_owner(gate_counts, got, sight, precision):
    owners = got.shape[0]
    return pl.pallas_call(
        owner_kernel,
        name="owner",
        in_specs=[smem, vmem, vmem, vmem],
        out_specs=[vmem, vmem],
        scratch_shapes=[pltpu.VMEM((owners // 8, lanes, 8 * lanes), bf16)],
        out_shape=[
            jax.ShapeDtypeStruct((owners, 4, lanes), f32),
            jax.ShapeDtypeStruct((1, sight.shape[2]), f32),
        ],
        compiler_params=room(24),
    )(gate_counts, got, sight, precision)


def call_scatter(returned, cells, slot, wind, wind_gradient, viscosity):
    _, cx, cy, nz = wind.shape
    tiles = cells.shape[0]
    half = returned.shape[0]
    return pl.pallas_call(
        scatter_kernel,
        name="scatter",
        in_specs=[vmem, vmem, vmem, hbm, hbm, hbm],
        out_specs=[vmem] * 8,
        scratch_shapes=[
            pltpu.VMEM((6 * half, 2 * lanes), bf16),
            pltpu.VMEM((3, tiles, tile), f32),
            pltpu.SMEM((tiles, tile), i32),
            pltpu.SemaphoreType.DMA((3,)),
            pltpu.SemaphoreType.DMA,
        ],
        out_shape=[
            jax.ShapeDtypeStruct((3, cx * cy, nz), f32),
            jax.ShapeDtypeStruct(wind.shape, f32),
            jax.ShapeDtypeStruct(wind_gradient.shape, f32),
            jax.ShapeDtypeStruct(viscosity.shape, f32),
            jax.ShapeDtypeStruct((3, cy, nz), f32),
            jax.ShapeDtypeStruct((3, cy, nz), f32),
            jax.ShapeDtypeStruct((3, cx, nz), f32),
            jax.ShapeDtypeStruct((3, cx, nz), f32),
        ],
        compiler_params=room(24),
    )(returned, cells, slot, held(wind), held(wind_gradient), held(viscosity))


def border_shapes(cx, cy, nz):
    return [(3, cy, nz), (3, cy, nz), (3, cx - 2, 8, nz), (3, cx - 2, 8, nz)]


def call_adjoint(pulled, wind, wind_gradient, viscosity):
    _, cx, cy, nz = wind.shape
    shapes = [(3, cx, cy, nz)] + border_shapes(cx, cy, nz)
    return pl.pallas_call(
        adjoint_kernel,
        name="adjoint",
        in_specs=[vmem] * 4,
        out_specs=[hbm] + [vmem] * 4,
        scratch_shapes=[pltpu.VMEM((3, cx + 2, cy, nz), f32), pltpu.SemaphoreType.DMA((cx,))],
        out_shape=[jax.ShapeDtypeStruct(shape, f32) for shape in shapes],
        compiler_params=room(24),
    )(pulled, wind, wind_gradient, viscosity)


def call_edges(result, sides, halo):
    _, cx, cy, nz = result.shape
    return pl.pallas_call(
        edge_kernel,
        name="edges",
        in_specs=[hbm] + [vmem] * 8,
        out_specs=hbm,
        scratch_shapes=[pltpu.VMEM(shape, f32) for shape in border_shapes(cx, cy, nz)]
        + [pltpu.SemaphoreType.DMA((4,))],
        out_shape=jax.ShapeDtypeStruct(result.shape, f32),
        input_output_aliases={0: 0},
        compiler_params=room(16),
    )(result, *sides, *halo)


def body(
    direction,
    wind,
    wind_gradient,
    viscosity,
    sample_owner,
    sample_cell,
    sample_gate,
    sight,
    gate_counts,
    precision,
):
    owners = lax.axis_size("track") * lax.axis_size("cross")
    names = ("track", "cross")
    xlo, xhi, ylo, yhi = call_border(direction)
    halo = (
        shifted(xhi, "track", 1),
        shifted(xlo, "track", -1),
        shifted(yhi, "cross", 1),
        shifted(ylo, "cross", -1),
    )
    cells, owner, gate = [
        v.reshape(-1, tile)
        for v in lax.sort(
            (sample_cell.reshape(-1), sample_owner.reshape(-1), sample_gate.reshape(-1)), num_keys=1, is_stable=False
        )
    ]
    slots, slot = call_sample(direction, halo, wind, wind_gradient, viscosity, cells, owner, gate, owners)
    got = lax.all_to_all(slots.reshape(owners, 4, lanes), names, split_axis=0, concat_axis=0, tiled=True)
    back, weighted = call_owner(gate_counts, got, sight, precision)
    returned = lax.all_to_all(back, names, split_axis=0, concat_axis=0, tiled=True)
    returned = returned.reshape(owners // 2, 2, 4, lanes)
    *taken, xlo, xhi, ylo, yhi = call_scatter(returned, cells, slot, wind, wind_gradient, viscosity)
    halo = (
        shifted(xhi, "track", 1),
        shifted(xlo, "track", -1),
        shifted(yhi, "cross", 1),
        shifted(ylo, "cross", -1),
    )
    result, *sides = call_adjoint(*taken)
    result = call_edges(result, sides, halo)
    return (result, weighted)


def solution(mesh):
    placed = (
        P(None, "track", "cross", None),
        P(None, "track", "cross", None),
        P(None, "track", "cross", None),
        P("track", "cross", None),
        P("track", "cross", None, None),
        P("track", "cross", None),
        P("track", "cross", None),
        P(None, ("track", "cross"), None),
        P(("track", "cross"), None),
        P(("track", "cross"), None, None),
    )
    return jax.shard_map(
        body,
        mesh=mesh,
        in_specs=placed,
        out_specs=(P(None, "track", "cross", None), P(("track", "cross"), None)),
        check_vma=False,
    )
```

```python
import jax
import jax.numpy as jnp
from jax import lax
from jax.experimental import pallas as pl
from jax.experimental.pallas import tpu as pltpu
from jax.sharding import PartitionSpec as P

time_step = 0.2
highest = lax.Precision.HIGHEST
tile = 256
lanes = 128
span = 64
strip = 16
batch = 2
row_bits = 8
f32 = jnp.float32
bf16 = jnp.bfloat16
i32 = jnp.int32


def split(value):
    head = value.astype(bf16)
    return head, (value - head.astype(f32)).astype(bf16)


def rows_equal(count, row):
    iota = lax.broadcasted_iota(i32, (count, row.shape[1]), 0)
    return iota == row


def pick(mask, value):
    return jnp.sum(jnp.where(mask, value, 0.0), axis=0, keepdims=True)


def onehot(count, row):
    iota = lax.broadcasted_iota(i32, (count, row.shape[1]), 0).astype(bf16)
    return jnp.where(iota == row.astype(f32).astype(bf16), jnp.ones((), bf16), jnp.zeros((), bf16))


def ones_at(mask):
    return jnp.where(mask, 1.0, 0.0).astype(bf16)


def dot_nt(a, b):
    return lax.dot_general(a, b, (((1,), (1,)), ((), ())), preferred_element_type=f32)


def dot_nn(a, b):
    return jnp.dot(a, b, preferred_element_type=f32)


def shift_rows(value, edge, by):
    count, wide = value.shape
    row = lax.broadcasted_iota(i32, (8, wide), 0)
    parts = [value[k : k + 8] for k in range(0, count, 8)]
    turned = [pltpu.roll(p, by % 8, 0) for p in parts]
    if by > 0:
        inner, beside = row == 0, [jnp.broadcast_to(edge, (8, wide))] + turned[:-1]
    else:
        inner, beside = row == 7, turned[1:] + [jnp.broadcast_to(edge, (8, wide))]
    return jnp.concatenate([jnp.where(inner, b, a) for a, b in zip(turned, beside)], axis=0)


def window(cell_s, t, rows):
    first = cell_s[t, 0] >> row_bits
    last = cell_s[t, tile - 1] >> row_bits
    base = jnp.minimum((first >> 4) << 4, rows - span)
    return pl.multiple_of(base, 16), last - base - span + 1


def each_tile(cell_s, tiles, rows, visit, more):
    def first(t, most):
        base, over = window(cell_s, t, rows)
        visit(t, base)
        return jnp.maximum(most, over)

    most = lax.fori_loop(0, tiles, first, i32(0), unroll=32)

    @pl.when(most > 0)
    def _():
        def rest(t, carry):
            base, over = window(cell_s, t, rows)

            def step(k, carry):
                least = base + k * span
                more(t, pl.multiple_of(jnp.minimum(least, rows - span), 16), least)
                return carry

            lax.fori_loop(1, 1 + (over + span - 1) // span, step, 0)
            return carry

        lax.fori_loop(0, tiles, rest, 0)


def divided(value, count):
    return value >> (count.bit_length() - 1), value & (count - 1)


def slot_parts(slot):
    return divided(slot, 2 * lanes)


def border_kernel(field_hbm, xlo_ref, xhi_ref, ylo_ref, yhi_ref, low_ref, high_ref, sems):
    nx, cy = field_hbm.shape[1], field_hbm.shape[2]
    copies = [
        pltpu.make_async_copy(field_hbm.at[:, :, pl.ds(0, 8)], low_ref, sems.at[0]),
        pltpu.make_async_copy(field_hbm.at[:, :, pl.ds(cy - 8, 8)], high_ref, sems.at[1]),
        pltpu.make_async_copy(field_hbm.at[:, 0], xlo_ref, sems.at[2]),
        pltpu.make_async_copy(field_hbm.at[:, nx - 1], xhi_ref, sems.at[3]),
    ]
    for copy in copies:
        copy.start()
    for copy, ref, into, at in ((copies[0], low_ref, ylo_ref, 0), (copies[1], high_ref, yhi_ref, 7)):
        copy.wait()
        for c in range(3):
            for x in range(nx):
                into[c, x : x + 1] = ref[c, x, at : at + 1]
    copies[2].wait()
    copies[3].wait()


def sample_kernel(
    field_hbm,
    xlo_ref,
    xhi_ref,
    ylo_ref,
    yhi_ref,
    wind_hbm,
    grad_hbm,
    visc_hbm,
    cell_ref,
    owner_ref,
    gate_ref,
    slots_ref,
    slot_ref,
    field_ref,
    wind_ref,
    grad_ref,
    visc_ref,
    plane_ref,
    value_ref,
    offset_ref,
    upper_ref,
    total_ref,
    cell_s,
    sems,
    cell_sem,
):
    nx, cy, nz = visc_ref.shape
    tiles = cell_ref.shape[0]
    owners = 2 * slots_ref.shape[0]
    rows = nx * cy

    def copies(k):
        part = pl.ds(k * batch, batch)
        return [
            pltpu.make_async_copy(field_hbm.at[:, part], field_ref.at[:, pl.ds(k * batch + 1, batch)], sems.at[0, k]),
            pltpu.make_async_copy(wind_hbm.at[:, part], wind_ref.at[:, part], sems.at[1, k]),
            pltpu.make_async_copy(grad_hbm.at[:, part], grad_ref.at[:, part], sems.at[2, k]),
            pltpu.make_async_copy(visc_hbm.at[part], visc_ref.at[part], sems.at[3, k]),
        ]

    list_cells = pltpu.make_async_copy(cell_ref, cell_s, cell_sem)
    list_cells.start()
    batches = nx // batch
    for k in range(batches):
        for copy in copies(k):
            copy.start()

    along, across = lax.axis_index("track"), lax.axis_index("cross")
    field_ref[:, 0] = jnp.where(along == 0, 0.0, xlo_ref[...])
    field_ref[:, nx + 1] = jnp.where(along == lax.axis_size("track") - 1, 0.0, xhi_ref[...])
    left_edge = across == 0
    right_edge = across == lax.axis_size("cross") - 1

    offset_ref[...] = jnp.zeros_like(offset_ref)
    a = lax.broadcasted_iota(i32, (tile, tile), 0)
    b = lax.broadcasted_iota(i32, (tile, tile), 1)
    upper_ref[...] = ones_at(a <= b)

    def rank(t, carry):
        own = owner_ref[pl.ds(t, 1), :]
        mask = rows_equal(owners, own)
        counts = dot_nn(ones_at(mask), upper_ref[...])
        offset = offset_ref[...]
        ranks = pick(mask, counts + jnp.concatenate([offset] * (tile // lanes), axis=1))
        slot_ref[pl.ds(t, 1), :] = own * lanes + ranks.astype(i32) - 1
        offset_ref[...] = offset + jnp.broadcast_to(counts[:, tile - 1 : tile], offset.shape)
        return carry

    lax.fori_loop(0, tiles, rank, 0, unroll=32)

    z_at = lax.broadcasted_iota(i32, (strip, nz), 1)

    def advance(x, carry):
        for y in range(0, cy, strip):
            part = pl.ds(y, strip)
            visc = time_step * visc_ref[x, part]
            wind = [(0.5 * time_step) * wind_ref[a, x, part] for a in range(3)]
            from_up, from_right, from_over = [visc - w for w in wind]
            from_down, from_left, from_under = [visc + w for w in wind]
            from_over = jnp.where(z_at == nz - 1, 0.0, from_over)
            from_under = jnp.where(z_at == 0, 0.0, from_under)
            own = 1.0 - 6.0 * visc
            here = [field_ref[c, x + 1, part] for c in range(3)]
            scaled = [time_step * f for f in here]
            for c in range(3):
                f = here[c]
                if y == 0:
                    before = jnp.where(left_edge, 0.0, ylo_ref[c, pl.ds(x, 1), :])
                else:
                    before = field_ref[c, x + 1, y - 1 : y]
                if y + strip == cy:
                    after = jnp.where(right_edge, 0.0, yhi_ref[c, pl.ds(x, 1), :])
                else:
                    after = field_ref[c, x + 1, y + strip : y + strip + 1]
                tangent = (
                    (own * f + from_up * field_ref[c, x + 2, part])
                    + (from_down * field_ref[c, x, part] + from_left * shift_rows(f, before, 1))
                    + (from_right * shift_rows(f, after, -1) + from_under * pltpu.roll(f, 1, 1))
                    + from_over * pltpu.roll(f, nz - 1, 1)
                ) - (
                    grad_ref[3 * c, x, part] * scaled[0]
                    + grad_ref[3 * c + 1, x, part] * scaled[1]
                    + grad_ref[3 * c + 2, x, part] * scaled[2]
                )
                head, rest = split(tangent)
                at = pl.multiple_of(x * cy + y, strip)
                plane_ref[c, pl.ds(at, strip), :nz] = head
                plane_ref[c, pl.ds(at, strip), nz:] = rest
        return carry

    copies(0)[0].wait()
    for k in range(batches):
        for copy in copies(k)[1:]:
            copy.wait()
        if k + 1 < batches:
            copies(k + 1)[0].wait()
        lax.fori_loop(k * batch, (k + 1) * batch, advance, 0)

    list_cells.wait()

    def find(t, begin, least):
        cells = cell_ref[pl.ds(t, 1), :]
        line, depth = divided(cells, nz)
        zs = onehot(nz, depth)
        mask = rows_equal(span, jnp.where(line >= least, line - begin, -1))
        block = jnp.concatenate(
            [plane_ref[c, pl.ds(begin, span), h * nz : (h + 1) * nz] for h in range(2) for c in range(3)], axis=0
        )
        found = dot_nn(block, zs)
        found = found[: 3 * span] + found[3 * span :]
        return [pick(mask, found[c * span : (c + 1) * span]) for c in range(3)]

    def gather(t, begin):
        for c, value in enumerate(find(t, begin, 0)):
            value_ref[c, pl.ds(t, 1), :] = value

    def gather_more(t, begin, least):
        for c, value in enumerate(find(t, begin, least)):
            value_ref[c, pl.ds(t, 1), :] += value

    each_tile(cell_s, tiles, rows, gather, gather_more)

    total_ref[...] = jnp.zeros_like(total_ref)
    half = owners // 2

    def add_tile(t, carry):
        line, column = slot_parts(slot_ref[pl.ds(t, 1), :])
        gate = gate_ref[pl.ds(t, 1), :]
        mask = rows_equal(half, line)
        columns = onehot(2 * lanes, column)
        _, low = divided(gate, lanes)
        parts = []
        for c in range(3):
            head, rest = split(value_ref[c, pl.ds(t, 1), :])
            parts.append((head.astype(f32), rest.astype(f32)))
        parts.append(((gate - low).astype(f32), low.astype(f32)))
        left = jnp.concatenate(
            [
                jnp.concatenate([jnp.where(mask, a, 0.0).astype(bf16), jnp.where(mask, b, 0.0).astype(bf16)], axis=1)
                for a, b in parts
            ],
            axis=0,
        )
        total_ref[...] += dot_nt(left, jnp.concatenate([columns, columns], axis=1))
        return carry

    lax.fori_loop(0, tiles, add_tile, 0, unroll=32)
    for c in range(4):
        for h in range(2):
            slots_ref[:, h, c, :] = total_ref[c * half : (c + 1) * half, h * lanes : (h + 1) * lanes]


def owner_kernel(counts_s, got_ref, sight_ref, precision_ref, back_ref, weighted_ref, gate_ref):
    sources = got_ref.shape[0]
    group = 8
    wide = group * lanes
    beams = counts_s.shape[1]

    def gathered(i):
        return jnp.concatenate([got_ref[i * group + j] for j in range(group)], axis=1)

    def beam_mask(gate):
        return rows_equal(beams, divided(gate, lanes)[0])

    def collect(i, acc):
        rows = gathered(i)
        gate = rows[3:4].astype(i32)
        gates = onehot(lanes, divided(gate, lanes)[1])
        gate_ref[i] = gates
        mask = beam_mask(gate)
        parts = []
        for k in range(3):
            head, rest = split(rows[k : k + 1])
            parts.append(jnp.where(mask, head.astype(f32), 0.0))
            parts.append(jnp.where(mask, rest.astype(f32), 0.0))
        left = jnp.concatenate(parts, axis=0).astype(bf16)
        return acc + dot_nt(left, gates)

    acc = lax.fori_loop(0, sources // group, collect, jnp.zeros((6 * beams, lanes), f32), unroll=8)
    sights = [
        jnp.concatenate([sight_ref[k, :, b * lanes : (b + 1) * lanes] for b in range(beams)], axis=0)
        for k in range(3)
    ]
    observed = jnp.zeros((beams, lanes), f32)
    for k in range(3):
        at = 2 * k * beams
        observed += sights[k] * (acc[at : at + beams] + acc[at + beams : at + 2 * beams])
    beam_at = lax.broadcasted_iota(i32, (beams, lanes), 0)
    gate_at = lax.broadcasted_iota(i32, (beams, lanes), 1)
    limit = jnp.zeros((beams, lanes), i32)
    for b in range(beams):
        limit = jnp.where(beam_at == b, counts_s[0, b], limit)
    live = jnp.where(gate_at < limit, 1.0, 0.0)
    weighted = live * jnp.dot(live * observed, precision_ref[0], precision=highest, preferred_element_type=f32)
    for b in range(beams):
        weighted_ref[:, b * lanes : (b + 1) * lanes] = weighted[b : b + 1]
    spread = jnp.concatenate([s * weighted for s in sights], axis=0)
    head = spread.astype(bf16).astype(f32)
    table = jnp.concatenate([head, spread - head], axis=0).astype(bf16)

    def give(i, carry):
        gate = gathered(i)[3:4].astype(i32)
        mask = beam_mask(gate)
        gates = gate_ref[i]
        found = dot_nn(table, gates)
        found = found[: 3 * beams] + found[3 * beams :]
        rows = jnp.concatenate(
            [pick(mask, found[k * beams : (k + 1) * beams]) for k in range(3)] + [jnp.zeros((1, wide), f32)], axis=0
        )
        for j in range(group):
            back_ref[i * group + j] = rows[:, j * lanes : (j + 1) * lanes]
        return carry

    lax.fori_loop(0, sources // group, give, 0, unroll=8)


def scatter_kernel(
    back_ref,
    cell_ref,
    slot_ref,
    wind_hbm,
    grad_hbm,
    visc_hbm,
    plane_ref,
    wind_ref,
    grad_ref,
    visc_ref,
    xlo_ref,
    xhi_ref,
    ylo_ref,
    yhi_ref,
    table_ref,
    value_ref,
    cell_s,
    sems,
    cell_sem,
):
    nx, cy, nz = visc_hbm.shape
    tiles = cell_ref.shape[0]
    half = back_ref.shape[0]
    rows = nx * cy
    list_cells = pltpu.make_async_copy(cell_ref, cell_s, cell_sem)
    list_cells.start()
    copies = [
        pltpu.make_async_copy(visc_hbm, visc_ref, sems.at[0]),
        pltpu.make_async_copy(wind_hbm, wind_ref, sems.at[1]),
        pltpu.make_async_copy(grad_hbm, grad_ref, sems.at[2]),
    ]
    for copy in copies:
        copy.start()
    for c in range(3):
        for h in range(2):
            head, rest = split(back_ref[:, h, c, :])
            table_ref[c * half : (c + 1) * half, h * lanes : (h + 1) * lanes] = head
            table_ref[(3 + c) * half : (4 + c) * half, h * lanes : (h + 1) * lanes] = rest
    plane_ref[...] = jnp.zeros_like(plane_ref)

    def restore(t, carry):
        line, column = slot_parts(slot_ref[pl.ds(t, 1), :])
        mask = rows_equal(half, line)
        columns = onehot(2 * lanes, column)
        found = dot_nn(table_ref[...], columns)
        found = found[: 3 * half] + found[3 * half :]
        for c in range(3):
            value_ref[c, pl.ds(t, 1), :] = pick(mask, found[c * half : (c + 1) * half])
        return carry

    lax.fori_loop(0, tiles, restore, 0, unroll=32)

    list_cells.wait()

    def put(t, begin, least):
        cells = cell_ref[pl.ds(t, 1), :]
        line, depth = divided(cells, nz)
        zs = onehot(nz, depth)
        mask = rows_equal(span, jnp.where(line >= least, line - begin, -1))
        heads, rests = [], []
        for c in range(3):
            head, rest = split(value_ref[c, pl.ds(t, 1), :])
            heads.append(jnp.where(mask, head.astype(f32), 0.0).astype(bf16))
            rests.append(jnp.where(mask, rest.astype(f32), 0.0).astype(bf16))
        added = dot_nt(jnp.concatenate(heads + rests, axis=0), zs)
        added = added[: 3 * span] + added[3 * span :]
        for c in range(3):
            plane_ref[c, pl.ds(begin, span), :] += added[c * span : (c + 1) * span]

    each_tile(cell_s, tiles, rows, lambda t, base: put(t, base, 0), put)

    for copy in copies:
        copy.wait()
    for x, ref, sign in ((0, xlo_ref, 1.0), (nx - 1, xhi_ref, -1.0)):
        passed = time_step * visc_ref[x] + (sign * 0.5 * time_step) * wind_ref[0, x]
        for c in range(3):
            ref[c] = passed * plane_ref[c, x * cy : (x + 1) * cy]
    for y, ref, sign in ((0, ylo_ref, 1.0), (cy - 1, yhi_ref, -1.0)):
        for x in range(nx):
            row = slice(y, y + 1)
            passed = time_step * visc_ref[x, row] + (sign * 0.5 * time_step) * wind_ref[1, x, row]
            for c in range(3):
                ref[c, x : x + 1] = passed * plane_ref[c, x * cy + y : x * cy + y + 1]


def adjoint_kernel(
    plane_ref, wind_ref, grad_ref, visc_ref, out_hbm, low_ref, high_ref, left_ref, right_ref, out_ref, sems
):
    nx, cy, nz = visc_ref.shape

    def write(x):
        return pltpu.make_async_copy(out_ref.at[:, x + 1], out_hbm.at[:, x], sems.at[x])

    z_at = lax.broadcasted_iota(i32, (strip, nz), 1)
    strips = cy // strip

    def advance(x, carry):
        def give(k):
            part = pl.ds(k * strip, strip)
            at = pl.multiple_of(x * cy + k * strip, strip)
            pulled = [plane_ref[c, pl.ds(at, strip), :] for c in range(3)]
            visc = time_step * visc_ref[x, part]
            wind = (0.5 * time_step) * wind_ref[1, x, part]
            to_left, to_right = visc + wind, visc - wind
            return pulled, visc, [to_left * p for p in pulled], [to_right * p for p in pulled]

        later = give(0)
        before = [jnp.zeros((1, nz), f32)] * 3
        for k in range(strips):
            pulled, visc, to_left, to_right = later
            part = pl.ds(k * strip, strip)
            after = [jnp.zeros((1, nz), f32)] * 3
            if k + 1 < strips:
                later = give(k + 1)
                after = [v[0:1] for v in later[2]]
            wind_x = (0.5 * time_step) * wind_ref[0, x, part]
            wind_z = (0.5 * time_step) * wind_ref[2, x, part]
            to_down, to_up = visc + wind_x, visc - wind_x
            to_under = jnp.where(z_at == 0, 0.0, visc + wind_z)
            to_over = jnp.where(z_at == nz - 1, 0.0, visc - wind_z)
            own = 1.0 - 6.0 * visc
            scaled = [time_step * p for p in pulled]
            for c in range(3):
                p = pulled[c]
                around = (shift_rows(to_left[c], after[c], -1) + shift_rows(to_right[c], before[c], 1)) + (
                    pltpu.roll(to_under * p, nz - 1, 1) + pltpu.roll(to_over * p, 1, 1)
                )
                gtr = (
                    grad_ref[c, x, part] * scaled[0]
                    + grad_ref[3 + c, x, part] * scaled[1]
                    + grad_ref[6 + c, x, part] * scaled[2]
                )
                out_ref[c, x, part] += to_down * p
                out_ref[c, x + 1, part] += own * p + (around - gtr)
                out_ref[c, x + 2, part] = to_up * p
            before = [v[strip - 1 : strip] for v in to_right]

        @pl.when(x > 0)
        def _():
            write(x - 1).start()

        return carry

    out_ref[:, 0:2] = jnp.zeros((3, 2, cy, nz), f32)
    lax.fori_loop(0, nx, advance, 0)
    low_ref[...] = out_ref[:, 1]
    high_ref[...] = out_ref[:, nx]
    left_ref[...] = out_ref[:, 2:nx, 0:8]
    right_ref[...] = out_ref[:, 2:nx, cy - 8 : cy]
    write(nx - 1).start()

    def end(x, carry):
        write(x).wait()
        return carry

    lax.fori_loop(0, nx, end, 0)


def edge_kernel(
    given_ref, low_ref, high_ref, left_ref, right_ref, xlo_ref, xhi_ref, ylo_ref, yhi_ref, out_ref, *scratch
):
    del given_ref
    *held_refs, sems = scratch
    along, across = lax.axis_index("track"), lax.axis_index("cross")
    last_along, last_across = lax.axis_size("track") - 1, lax.axis_size("cross") - 1
    nx, cy = out_ref.shape[1], out_ref.shape[2]
    inner = nx - 2
    left_edge, right_edge = across == 0, across == last_across
    places = [
        out_ref.at[:, 0],
        out_ref.at[:, nx - 1],
        out_ref.at[:, pl.ds(1, inner), pl.ds(0, 8)],
        out_ref.at[:, pl.ds(1, inner), pl.ds(cy - 8, 8)],
    ]
    writes = [pltpu.make_async_copy(a, b, sems.at[i]) for i, (a, b) in enumerate(zip(held_refs, places))]
    sides = (
        (0, held_refs[0], low_ref, xlo_ref, along == 0),
        (nx - 1, held_refs[1], high_ref, xhi_ref, along == last_along),
    )
    for i, (x, ref, own, halo, edge) in enumerate(sides):
        for c in range(3):
            ref[c] = own[c] + jnp.where(edge, 0.0, halo[c])
            ref[c, 0:1] += jnp.where(left_edge, 0.0, ylo_ref[c, x : x + 1])
            ref[c, cy - 1 : cy] += jnp.where(right_edge, 0.0, yhi_ref[c, x : x + 1])
        writes[i].start()
    row_at = lax.broadcasted_iota(i32, (8, out_ref.shape[3]), 0)
    for i, row, own, halo, edge in ((2, 0, left_ref, ylo_ref, left_edge), (3, 7, right_ref, yhi_ref, right_edge)):
        ref = held_refs[i]
        here = (row_at == row) & jnp.logical_not(edge)
        for c in range(3):
            for k in range(inner):
                ref[c, k] = own[c, k] + jnp.where(here, halo[c, k + 1 : k + 2], 0.0)
        writes[i].start()
    for write in writes:
        write.wait()


def shifted(value, axis, by):
    count = lax.axis_size(axis)
    return lax.ppermute(value, axis, [(i, (i + by) % count) for i in range(count)])


vmem = pl.BlockSpec(memory_space=pltpu.VMEM)
smem = pl.BlockSpec(memory_space=pltpu.SMEM)
hbm = pl.BlockSpec(memory_space=pltpu.HBM)


def held(value):
    return pltpu.with_memory_space_constraint(value, pltpu.HBM)


def room(mib):
    return pltpu.CompilerParams(vmem_limit_bytes=mib << 20)


def call_border(field):
    _, cx, cy, nz = field.shape
    return pl.pallas_call(
        border_kernel,
        name="border",
        in_specs=[hbm],
        out_specs=[vmem] * 4,
        scratch_shapes=[
            pltpu.VMEM((3, cx, 8, nz), f32),
            pltpu.VMEM((3, cx, 8, nz), f32),
            pltpu.SemaphoreType.DMA((4,)),
        ],
        out_shape=[
            jax.ShapeDtypeStruct((3, cy, nz), f32),
            jax.ShapeDtypeStruct((3, cy, nz), f32),
            jax.ShapeDtypeStruct((3, cx, nz), f32),
            jax.ShapeDtypeStruct((3, cx, nz), f32),
        ],
        compiler_params=room(8),
    )(held(field))


def call_sample(direction, halo, wind, wind_gradient, viscosity, cells, owner, gate, owners):
    _, cx, cy, nz = direction.shape
    tiles = cells.shape[0]
    return pl.pallas_call(
        sample_kernel,
        name="sample",
        in_specs=[hbm, vmem, vmem, vmem, vmem, hbm, hbm, hbm, vmem, vmem, vmem],
        out_specs=[vmem, vmem],
        scratch_shapes=[
            pltpu.VMEM((3, cx + 2, cy, nz), f32),
            pltpu.VMEM((3, cx, cy, nz), f32),
            pltpu.VMEM((9, cx, cy, nz), f32),
            pltpu.VMEM((cx, cy, nz), f32),
            pltpu.VMEM((3, cx * cy, 2 * nz), bf16),
            pltpu.VMEM((3, tiles, tile), f32),
            pltpu.VMEM((owners, lanes), f32),
            pltpu.VMEM((tile, tile), bf16),
            pltpu.VMEM((2 * owners, 2 * lanes), f32),
            pltpu.SMEM((tiles, tile), i32),
            pltpu.SemaphoreType.DMA((4, cx)),
            pltpu.SemaphoreType.DMA,
        ],
        out_shape=[
            jax.ShapeDtypeStruct((owners // 2, 2, 4, lanes), f32),
            jax.ShapeDtypeStruct((tiles, tile), i32),
        ],
        compiler_params=room(40),
    )(held(direction), *halo, held(wind), held(wind_gradient), held(viscosity), cells, owner, gate)


def call_owner(gate_counts, got, sight, precision):
    owners = got.shape[0]
    return pl.pallas_call(
        owner_kernel,
        name="owner",
        in_specs=[smem, vmem, vmem, vmem],
        out_specs=[vmem, vmem],
        scratch_shapes=[pltpu.VMEM((owners // 8, lanes, 8 * lanes), bf16)],
        out_shape=[
            jax.ShapeDtypeStruct((owners, 4, lanes), f32),
            jax.ShapeDtypeStruct((1, sight.shape[2]), f32),
        ],
        compiler_params=room(24),
    )(gate_counts, got, sight, precision)


def call_scatter(returned, cells, slot, wind, wind_gradient, viscosity):
    _, cx, cy, nz = wind.shape
    tiles = cells.shape[0]
    half = returned.shape[0]
    return pl.pallas_call(
        scatter_kernel,
        name="scatter",
        in_specs=[vmem, vmem, vmem, hbm, hbm, hbm],
        out_specs=[vmem] * 8,
        scratch_shapes=[
            pltpu.VMEM((6 * half, 2 * lanes), bf16),
            pltpu.VMEM((3, tiles, tile), f32),
            pltpu.SMEM((tiles, tile), i32),
            pltpu.SemaphoreType.DMA((3,)),
            pltpu.SemaphoreType.DMA,
        ],
        out_shape=[
            jax.ShapeDtypeStruct((3, cx * cy, nz), f32),
            jax.ShapeDtypeStruct(wind.shape, f32),
            jax.ShapeDtypeStruct(wind_gradient.shape, f32),
            jax.ShapeDtypeStruct(viscosity.shape, f32),
            jax.ShapeDtypeStruct((3, cy, nz), f32),
            jax.ShapeDtypeStruct((3, cy, nz), f32),
            jax.ShapeDtypeStruct((3, cx, nz), f32),
            jax.ShapeDtypeStruct((3, cx, nz), f32),
        ],
        compiler_params=room(24),
    )(returned, cells, slot, held(wind), held(wind_gradient), held(viscosity))


def border_shapes(cx, cy, nz):
    return [(3, cy, nz), (3, cy, nz), (3, cx - 2, 8, nz), (3, cx - 2, 8, nz)]


def call_adjoint(pulled, wind, wind_gradient, viscosity):
    _, cx, cy, nz = wind.shape
    shapes = [(3, cx, cy, nz)] + border_shapes(cx, cy, nz)
    return pl.pallas_call(
        adjoint_kernel,
        name="adjoint",
        in_specs=[vmem] * 4,
        out_specs=[hbm] + [vmem] * 4,
        scratch_shapes=[pltpu.VMEM((3, cx + 2, cy, nz), f32), pltpu.SemaphoreType.DMA((cx,))],
        out_shape=[jax.ShapeDtypeStruct(shape, f32) for shape in shapes],
        compiler_params=room(24),
    )(pulled, wind, wind_gradient, viscosity)


def call_edges(result, sides, halo):
    _, cx, cy, nz = result.shape
    return pl.pallas_call(
        edge_kernel,
        name="edges",
        in_specs=[hbm] + [vmem] * 8,
        out_specs=hbm,
        scratch_shapes=[pltpu.VMEM(shape, f32) for shape in border_shapes(cx, cy, nz)]
        + [pltpu.SemaphoreType.DMA((4,))],
        out_shape=jax.ShapeDtypeStruct(result.shape, f32),
        input_output_aliases={0: 0},
        compiler_params=room(16),
    )(result, *sides, *halo)


def body(
    direction,
    wind,
    wind_gradient,
    viscosity,
    sample_owner,
    sample_cell,
    sample_gate,
    sight,
    gate_counts,
    precision,
):
    owners = lax.axis_size("track") * lax.axis_size("cross")
    names = ("track", "cross")
    xlo, xhi, ylo, yhi = call_border(direction)
    halo = (
        shifted(xhi, "track", 1),
        shifted(xlo, "track", -1),
        shifted(yhi, "cross", 1),
        shifted(ylo, "cross", -1),
    )
    cells, owner, gate = [
        v.reshape(-1, tile)
        for v in lax.sort(
            (sample_cell.reshape(-1), sample_owner.reshape(-1), sample_gate.reshape(-1)), num_keys=1, is_stable=False
        )
    ]
    slots, slot = call_sample(direction, halo, wind, wind_gradient, viscosity, cells, owner, gate, owners)
    got = lax.all_to_all(slots.reshape(owners, 4, lanes), names, split_axis=0, concat_axis=0, tiled=True)
    back, weighted = call_owner(gate_counts, got, sight, precision)
    returned = lax.all_to_all(back, names, split_axis=0, concat_axis=0, tiled=True)
    returned = returned.reshape(owners // 2, 2, 4, lanes)
    *taken, xlo, xhi, ylo, yhi = call_scatter(returned, cells, slot, wind, wind_gradient, viscosity)
    halo = (
        shifted(xhi, "track", 1),
        shifted(xlo, "track", -1),
        shifted(yhi, "cross", 1),
        shifted(ylo, "cross", -1),
    )
    result, *sides = call_adjoint(*taken)
    result = call_edges(result, sides, halo)
    return (result, weighted)


def solution(mesh):
    placed = (
        P(None, "track", "cross", None),
        P(None, "track", "cross", None),
        P(None, "track", "cross", None),
        P("track", "cross", None),
        P("track", "cross", None, None),
        P("track", "cross", None),
        P("track", "cross", None),
        P(None, ("track", "cross"), None),
        P(("track", "cross"), None),
        P(("track", "cross"), None, None),
    )
    return jax.shard_map(
        body,
        mesh=mesh,
        in_specs=placed,
        out_specs=(P(None, "track", "cross", None), P(("track", "cross"), None)),
        check_vma=False,
    )
```

```python
import jax
import jax.numpy as jnp
from jax import lax
from jax.experimental import pallas as pl
from jax.experimental.pallas import tpu as pltpu
from jax.sharding import PartitionSpec as P

time_step = 0.2
highest = lax.Precision.HIGHEST
tile = 256
lanes = 128
span = 64
strip = 16
batch = 2
row_bits = 8
f32 = jnp.float32
bf16 = jnp.bfloat16
i32 = jnp.int32


def split(value):
    head = value.astype(bf16)
    return head, (value - head.astype(f32)).astype(bf16)


def rows_equal(count, row):
    iota = lax.broadcasted_iota(i32, (count, row.shape[1]), 0)
    return iota == row


def pick(mask, value):
    return jnp.sum(jnp.where(mask, value, 0.0), axis=0, keepdims=True)


def onehot(count, row):
    iota = lax.broadcasted_iota(i32, (count, row.shape[1]), 0).astype(bf16)
    return jnp.where(iota == row.astype(f32).astype(bf16), jnp.ones((), bf16), jnp.zeros((), bf16))


def ones_at(mask):
    return jnp.where(mask, 1.0, 0.0).astype(bf16)


def dot_nt(a, b):
    return lax.dot_general(a, b, (((1,), (1,)), ((), ())), preferred_element_type=f32)


def dot_nn(a, b):
    return jnp.dot(a, b, preferred_element_type=f32)


def shift_rows(value, edge, by):
    count, wide = value.shape
    row = lax.broadcasted_iota(i32, (8, wide), 0)
    parts = [value[k : k + 8] for k in range(0, count, 8)]
    turned = [pltpu.roll(p, by % 8, 0) for p in parts]
    if by > 0:
        inner, beside = row == 0, [jnp.broadcast_to(edge, (8, wide))] + turned[:-1]
    else:
        inner, beside = row == 7, turned[1:] + [jnp.broadcast_to(edge, (8, wide))]
    return jnp.concatenate([jnp.where(inner, b, a) for a, b in zip(turned, beside)], axis=0)


def window(cell_s, t, rows):
    first = cell_s[t, 0] >> row_bits
    last = cell_s[t, tile - 1] >> row_bits
    base = jnp.minimum((first >> 4) << 4, rows - span)
    return pl.multiple_of(base, 16), last - base - span + 1


def each_tile(cell_s, tiles, rows, visit, more):
    def first(t, most):
        base, over = window(cell_s, t, rows)
        visit(t, base)
        return jnp.maximum(most, over)

    most = lax.fori_loop(0, tiles, first, i32(0), unroll=32)

    @pl.when(most > 0)
    def _():
        def rest(t, carry):
            base, over = window(cell_s, t, rows)

            def step(k, carry):
                least = base + k * span
                more(t, pl.multiple_of(jnp.minimum(least, rows - span), 16), least)
                return carry

            lax.fori_loop(1, 1 + (over + span - 1) // span, step, 0)
            return carry

        lax.fori_loop(0, tiles, rest, 0)


def divided(value, count):
    return value >> (count.bit_length() - 1), value & (count - 1)


def slot_parts(slot):
    return divided(slot, 2 * lanes)


def border_kernel(field_hbm, xlo_ref, xhi_ref, ylo_ref, yhi_ref, low_ref, high_ref, sems):
    nx, cy = field_hbm.shape[1], field_hbm.shape[2]
    copies = [
        pltpu.make_async_copy(field_hbm.at[:, :, pl.ds(0, 8)], low_ref, sems.at[0]),
        pltpu.make_async_copy(field_hbm.at[:, :, pl.ds(cy - 8, 8)], high_ref, sems.at[1]),
        pltpu.make_async_copy(field_hbm.at[:, 0], xlo_ref, sems.at[2]),
        pltpu.make_async_copy(field_hbm.at[:, nx - 1], xhi_ref, sems.at[3]),
    ]
    for copy in copies:
        copy.start()
    for copy, ref, into, at in ((copies[0], low_ref, ylo_ref, 0), (copies[1], high_ref, yhi_ref, 7)):
        copy.wait()
        for c in range(3):
            for x in range(nx):
                into[c, x : x + 1] = ref[c, x, at : at + 1]
    copies[2].wait()
    copies[3].wait()


def sample_kernel(
    field_hbm,
    xlo_ref,
    xhi_ref,
    ylo_ref,
    yhi_ref,
    wind_hbm,
    grad_hbm,
    visc_hbm,
    cell_ref,
    owner_ref,
    gate_ref,
    slots_ref,
    slot_ref,
    field_ref,
    wind_ref,
    grad_ref,
    visc_ref,
    plane_ref,
    value_ref,
    offset_ref,
    upper_ref,
    total_ref,
    cell_s,
    sems,
    cell_sem,
):
    nx, cy, nz = visc_ref.shape
    tiles = cell_ref.shape[0]
    owners = 2 * slots_ref.shape[1]
    rows = nx * cy

    def copies(k):
        part = pl.ds(k * batch, batch)
        return [
            pltpu.make_async_copy(field_hbm.at[:, part], field_ref.at[:, pl.ds(k * batch + 1, batch)], sems.at[0, k]),
            pltpu.make_async_copy(wind_hbm.at[:, part], wind_ref.at[:, part], sems.at[1, k]),
            pltpu.make_async_copy(grad_hbm.at[:, part], grad_ref.at[:, part], sems.at[2, k]),
            pltpu.make_async_copy(visc_hbm.at[part], visc_ref.at[part], sems.at[3, k]),
        ]

    list_cells = pltpu.make_async_copy(cell_ref, cell_s, cell_sem)
    list_cells.start()
    batches = nx // batch
    for k in range(batches):
        for copy in copies(k):
            copy.start()

    along, across = lax.axis_index("track"), lax.axis_index("cross")
    field_ref[:, 0] = jnp.where(along == 0, 0.0, xlo_ref[...])
    field_ref[:, nx + 1] = jnp.where(along == lax.axis_size("track") - 1, 0.0, xhi_ref[...])
    left_edge = across == 0
    right_edge = across == lax.axis_size("cross") - 1

    offset_ref[...] = jnp.zeros_like(offset_ref)
    a = lax.broadcasted_iota(i32, (tile, tile), 0)
    b = lax.broadcasted_iota(i32, (tile, tile), 1)
    upper_ref[...] = ones_at(a <= b)

    def rank(t, carry):
        own = owner_ref[pl.ds(t, 1), :]
        mask = rows_equal(owners, own)
        counts = dot_nn(ones_at(mask), upper_ref[...])
        offset = offset_ref[...]
        ranks = pick(mask, counts + jnp.concatenate([offset] * (tile // lanes), axis=1))
        high, line = divided(own, owners // 2)
        slot_ref[pl.ds(t, 1), :] = (2 * line + high) * lanes + ranks.astype(i32) - 1
        offset_ref[...] = offset + jnp.broadcast_to(counts[:, tile - 1 : tile], offset.shape)
        return carry

    lax.fori_loop(0, tiles, rank, 0, unroll=32)

    z_at = lax.broadcasted_iota(i32, (strip, nz), 1)

    def advance(x, carry):
        for y in range(0, cy, strip):
            part = pl.ds(y, strip)
            visc = time_step * visc_ref[x, part]
            wind = [(0.5 * time_step) * wind_ref[a, x, part] for a in range(3)]
            from_up, from_right, from_over = [visc - w for w in wind]
            from_down, from_left, from_under = [visc + w for w in wind]
            from_over = jnp.where(z_at == nz - 1, 0.0, from_over)
            from_under = jnp.where(z_at == 0, 0.0, from_under)
            own = 1.0 - 6.0 * visc
            here = [field_ref[c, x + 1, part] for c in range(3)]
            scaled = [time_step * f for f in here]
            for c in range(3):
                f = here[c]
                if y == 0:
                    before = jnp.where(left_edge, 0.0, ylo_ref[c, pl.ds(x, 1), :])
                else:
                    before = field_ref[c, x + 1, y - 1 : y]
                if y + strip == cy:
                    after = jnp.where(right_edge, 0.0, yhi_ref[c, pl.ds(x, 1), :])
                else:
                    after = field_ref[c, x + 1, y + strip : y + strip + 1]
                tangent = (
                    (own * f + from_up * field_ref[c, x + 2, part])
                    + (from_down * field_ref[c, x, part] + from_left * shift_rows(f, before, 1))
                    + (from_right * shift_rows(f, after, -1) + from_under * pltpu.roll(f, 1, 1))
                    + from_over * pltpu.roll(f, nz - 1, 1)
                ) - (
                    grad_ref[3 * c, x, part] * scaled[0]
                    + grad_ref[3 * c + 1, x, part] * scaled[1]
                    + grad_ref[3 * c + 2, x, part] * scaled[2]
                )
                head, rest = split(tangent)
                at = pl.multiple_of(x * cy + y, strip)
                plane_ref[c, pl.ds(at, strip), :nz] = head
                plane_ref[c, pl.ds(at, strip), nz:] = rest
        return carry

    copies(0)[0].wait()
    for k in range(batches):
        for copy in copies(k)[1:]:
            copy.wait()
        if k + 1 < batches:
            copies(k + 1)[0].wait()
        lax.fori_loop(k * batch, (k + 1) * batch, advance, 0)

    list_cells.wait()

    def find(t, begin, least):
        cells = cell_ref[pl.ds(t, 1), :]
        line, depth = divided(cells, nz)
        zs = onehot(nz, depth)
        mask = rows_equal(span, jnp.where(line >= least, line - begin, -1))
        block = jnp.concatenate(
            [plane_ref[c, pl.ds(begin, span), h * nz : (h + 1) * nz] for h in range(2) for c in range(3)], axis=0
        )
        found = dot_nn(block, zs)
        found = found[: 3 * span] + found[3 * span :]
        return [pick(mask, found[c * span : (c + 1) * span]) for c in range(3)]

    def gather(t, begin):
        for c, value in enumerate(find(t, begin, 0)):
            value_ref[c, pl.ds(t, 1), :] = value

    def gather_more(t, begin, least):
        for c, value in enumerate(find(t, begin, least)):
            value_ref[c, pl.ds(t, 1), :] += value

    each_tile(cell_s, tiles, rows, gather, gather_more)

    total_ref[...] = jnp.zeros_like(total_ref)
    half = owners // 2

    def add_tile(t, carry):
        line, column = slot_parts(slot_ref[pl.ds(t, 1), :])
        gate = gate_ref[pl.ds(t, 1), :]
        mask = rows_equal(half, line)
        columns = onehot(2 * lanes, column)
        _, low = divided(gate, lanes)
        parts = []
        for c in range(3):
            head, rest = split(value_ref[c, pl.ds(t, 1), :])
            parts.append((head.astype(f32), rest.astype(f32)))
        parts.append(((gate - low).astype(f32), low.astype(f32)))
        left = jnp.concatenate(
            [
                jnp.concatenate([jnp.where(mask, a, 0.0).astype(bf16), jnp.where(mask, b, 0.0).astype(bf16)], axis=1)
                for a, b in parts
            ],
            axis=0,
        )
        total_ref[...] += dot_nt(left, jnp.concatenate([columns, columns], axis=1))
        return carry

    lax.fori_loop(0, tiles, add_tile, 0, unroll=32)
    for c in range(4):
        for h in range(2):
            slots_ref[h, :, c, :] = total_ref[c * half : (c + 1) * half, h * lanes : (h + 1) * lanes]


def owner_kernel(counts_s, got_ref, sight_ref, precision_ref, back_ref, weighted_ref, gate_ref):
    sources = got_ref.shape[0]
    group = 8
    wide = group * lanes
    beams = counts_s.shape[1]

    def gathered(i):
        return jnp.concatenate([got_ref[i * group + j] for j in range(group)], axis=1)

    def beam_mask(gate):
        return rows_equal(beams, divided(gate, lanes)[0])

    def collect(i, acc):
        rows = gathered(i)
        gate = rows[3:4].astype(i32)
        gates = onehot(lanes, divided(gate, lanes)[1])
        gate_ref[i] = gates
        mask = beam_mask(gate)
        parts = []
        for k in range(3):
            head, rest = split(rows[k : k + 1])
            parts.append(jnp.where(mask, head.astype(f32), 0.0))
            parts.append(jnp.where(mask, rest.astype(f32), 0.0))
        left = jnp.concatenate(parts, axis=0).astype(bf16)
        return acc + dot_nt(left, gates)

    acc = lax.fori_loop(0, sources // group, collect, jnp.zeros((6 * beams, lanes), f32), unroll=8)
    sights = [
        jnp.concatenate([sight_ref[k, :, b * lanes : (b + 1) * lanes] for b in range(beams)], axis=0)
        for k in range(3)
    ]
    observed = jnp.zeros((beams, lanes), f32)
    for k in range(3):
        at = 2 * k * beams
        observed += sights[k] * (acc[at : at + beams] + acc[at + beams : at + 2 * beams])
    beam_at = lax.broadcasted_iota(i32, (beams, lanes), 0)
    gate_at = lax.broadcasted_iota(i32, (beams, lanes), 1)
    limit = jnp.zeros((beams, lanes), i32)
    for b in range(beams):
        limit = jnp.where(beam_at == b, counts_s[0, b], limit)
    live = jnp.where(gate_at < limit, 1.0, 0.0)
    weighted = live * jnp.dot(live * observed, precision_ref[0], precision=highest, preferred_element_type=f32)
    for b in range(beams):
        weighted_ref[:, b * lanes : (b + 1) * lanes] = weighted[b : b + 1]
    spread = jnp.concatenate([s * weighted for s in sights], axis=0)
    head = spread.astype(bf16).astype(f32)
    table = jnp.concatenate([head, spread - head], axis=0).astype(bf16)

    def give(i, carry):
        gate = gathered(i)[3:4].astype(i32)
        mask = beam_mask(gate)
        gates = gate_ref[i]
        found = dot_nn(table, gates)
        found = found[: 3 * beams] + found[3 * beams :]
        for k in range(3):
            row = pick(mask, found[k * beams : (k + 1) * beams])
            for j in range(group):
                back_ref[i * group + j, :, k * lanes : (k + 1) * lanes] = row[:, j * lanes : (j + 1) * lanes]
        return carry

    lax.fori_loop(0, sources // group, give, 0, unroll=8)


def scatter_kernel(
    back_ref,
    cell_ref,
    slot_ref,
    wind_hbm,
    grad_hbm,
    visc_hbm,
    plane_ref,
    wind_ref,
    grad_ref,
    visc_ref,
    xlo_ref,
    xhi_ref,
    ylo_ref,
    yhi_ref,
    table_ref,
    value_ref,
    cell_s,
    sems,
    cell_sem,
):
    nx, cy, nz = visc_hbm.shape
    tiles = cell_ref.shape[0]
    half = back_ref.shape[0] // 2
    rows = nx * cy
    list_cells = pltpu.make_async_copy(cell_ref, cell_s, cell_sem)
    list_cells.start()
    copies = [
        pltpu.make_async_copy(visc_hbm, visc_ref, sems.at[0]),
        pltpu.make_async_copy(wind_hbm, wind_ref, sems.at[1]),
        pltpu.make_async_copy(grad_hbm, grad_ref, sems.at[2]),
    ]
    for copy in copies:
        copy.start()
    for c in range(3):
        for h in range(2):
            head, rest = split(back_ref[h * half : (h + 1) * half, 0, c * lanes : (c + 1) * lanes])
            table_ref[c * half : (c + 1) * half, h * lanes : (h + 1) * lanes] = head
            table_ref[(3 + c) * half : (4 + c) * half, h * lanes : (h + 1) * lanes] = rest
    plane_ref[...] = jnp.zeros_like(plane_ref)

    def restore(t, carry):
        line, column = slot_parts(slot_ref[pl.ds(t, 1), :])
        mask = rows_equal(half, line)
        columns = onehot(2 * lanes, column)
        found = dot_nn(table_ref[...], columns)
        found = found[: 3 * half] + found[3 * half :]
        for c in range(3):
            value_ref[c, pl.ds(t, 1), :] = pick(mask, found[c * half : (c + 1) * half])
        return carry

    lax.fori_loop(0, tiles, restore, 0, unroll=32)

    list_cells.wait()

    def put(t, begin, least):
        cells = cell_ref[pl.ds(t, 1), :]
        line, depth = divided(cells, nz)
        zs = onehot(nz, depth)
        mask = rows_equal(span, jnp.where(line >= least, line - begin, -1))
        heads, rests = [], []
        for c in range(3):
            head, rest = split(value_ref[c, pl.ds(t, 1), :])
            heads.append(jnp.where(mask, head.astype(f32), 0.0).astype(bf16))
            rests.append(jnp.where(mask, rest.astype(f32), 0.0).astype(bf16))
        added = dot_nt(jnp.concatenate(heads + rests, axis=0), zs)
        added = added[: 3 * span] + added[3 * span :]
        for c in range(3):
            plane_ref[c, pl.ds(begin, span), :] += added[c * span : (c + 1) * span]

    each_tile(cell_s, tiles, rows, lambda t, base: put(t, base, 0), put)

    for copy in copies:
        copy.wait()
    for x, ref, sign in ((0, xlo_ref, 1.0), (nx - 1, xhi_ref, -1.0)):
        passed = time_step * visc_ref[x] + (sign * 0.5 * time_step) * wind_ref[0, x]
        for c in range(3):
            ref[c] = passed * plane_ref[c, x * cy : (x + 1) * cy]
    for y, ref, sign in ((0, ylo_ref, 1.0), (cy - 1, yhi_ref, -1.0)):
        for x in range(nx):
            row = slice(y, y + 1)
            passed = time_step * visc_ref[x, row] + (sign * 0.5 * time_step) * wind_ref[1, x, row]
            for c in range(3):
                ref[c, x : x + 1] = passed * plane_ref[c, x * cy + y : x * cy + y + 1]


def adjoint_kernel(
    plane_ref, wind_ref, grad_ref, visc_ref, out_hbm, low_ref, high_ref, left_ref, right_ref, out_ref, sems
):
    nx, cy, nz = visc_ref.shape

    def write(x):
        return pltpu.make_async_copy(out_ref.at[:, x + 1], out_hbm.at[:, x], sems.at[x])

    z_at = lax.broadcasted_iota(i32, (strip, nz), 1)
    strips = cy // strip

    def advance(x, carry):
        def give(k):
            part = pl.ds(k * strip, strip)
            at = pl.multiple_of(x * cy + k * strip, strip)
            pulled = [plane_ref[c, pl.ds(at, strip), :] for c in range(3)]
            visc = time_step * visc_ref[x, part]
            wind = (0.5 * time_step) * wind_ref[1, x, part]
            to_left, to_right = visc + wind, visc - wind
            return pulled, visc, [to_left * p for p in pulled], [to_right * p for p in pulled]

        later = give(0)
        before = [jnp.zeros((1, nz), f32)] * 3
        for k in range(strips):
            pulled, visc, to_left, to_right = later
            part = pl.ds(k * strip, strip)
            after = [jnp.zeros((1, nz), f32)] * 3
            if k + 1 < strips:
                later = give(k + 1)
                after = [v[0:1] for v in later[2]]
            wind_x = (0.5 * time_step) * wind_ref[0, x, part]
            wind_z = (0.5 * time_step) * wind_ref[2, x, part]
            to_down, to_up = visc + wind_x, visc - wind_x
            to_under = jnp.where(z_at == 0, 0.0, visc + wind_z)
            to_over = jnp.where(z_at == nz - 1, 0.0, visc - wind_z)
            own = 1.0 - 6.0 * visc
            scaled = [time_step * p for p in pulled]
            for c in range(3):
                p = pulled[c]
                around = (shift_rows(to_left[c], after[c], -1) + shift_rows(to_right[c], before[c], 1)) + (
                    pltpu.roll(to_under * p, nz - 1, 1) + pltpu.roll(to_over * p, 1, 1)
                )
                gtr = (
                    grad_ref[c, x, part] * scaled[0]
                    + grad_ref[3 + c, x, part] * scaled[1]
                    + grad_ref[6 + c, x, part] * scaled[2]
                )
                out_ref[c, x, part] += to_down * p
                out_ref[c, x + 1, part] += own * p + (around - gtr)
                out_ref[c, x + 2, part] = to_up * p
            before = [v[strip - 1 : strip] for v in to_right]

        @pl.when(x > 0)
        def _():
            write(x - 1).start()

        return carry

    out_ref[:, 0:2] = jnp.zeros((3, 2, cy, nz), f32)
    lax.fori_loop(0, nx, advance, 0)
    low_ref[...] = out_ref[:, 1]
    high_ref[...] = out_ref[:, nx]
    left_ref[...] = out_ref[:, 2:nx, 0:8]
    right_ref[...] = out_ref[:, 2:nx, cy - 8 : cy]
    write(nx - 1).start()

    def end(x, carry):
        write(x).wait()
        return carry

    lax.fori_loop(0, nx, end, 0)


def edge_kernel(
    given_ref, low_ref, high_ref, left_ref, right_ref, xlo_ref, xhi_ref, ylo_ref, yhi_ref, out_ref, *scratch
):
    del given_ref
    *held_refs, sems = scratch
    along, across = lax.axis_index("track"), lax.axis_index("cross")
    last_along, last_across = lax.axis_size("track") - 1, lax.axis_size("cross") - 1
    nx, cy = out_ref.shape[1], out_ref.shape[2]
    inner = nx - 2
    left_edge, right_edge = across == 0, across == last_across
    places = [
        out_ref.at[:, 0],
        out_ref.at[:, nx - 1],
        out_ref.at[:, pl.ds(1, inner), pl.ds(0, 8)],
        out_ref.at[:, pl.ds(1, inner), pl.ds(cy - 8, 8)],
    ]
    writes = [pltpu.make_async_copy(a, b, sems.at[i]) for i, (a, b) in enumerate(zip(held_refs, places))]
    sides = (
        (0, held_refs[0], low_ref, xlo_ref, along == 0),
        (nx - 1, held_refs[1], high_ref, xhi_ref, along == last_along),
    )
    for i, (x, ref, own, halo, edge) in enumerate(sides):
        for c in range(3):
            ref[c] = own[c] + jnp.where(edge, 0.0, halo[c])
            ref[c, 0:1] += jnp.where(left_edge, 0.0, ylo_ref[c, x : x + 1])
            ref[c, cy - 1 : cy] += jnp.where(right_edge, 0.0, yhi_ref[c, x : x + 1])
        writes[i].start()
    row_at = lax.broadcasted_iota(i32, (8, out_ref.shape[3]), 0)
    for i, row, own, halo, edge in ((2, 0, left_ref, ylo_ref, left_edge), (3, 7, right_ref, yhi_ref, right_edge)):
        ref = held_refs[i]
        here = (row_at == row) & jnp.logical_not(edge)
        for c in range(3):
            for k in range(inner):
                ref[c, k] = own[c, k] + jnp.where(here, halo[c, k + 1 : k + 2], 0.0)
        writes[i].start()
    for write in writes:
        write.wait()


def shifted(value, axis, by):
    count = lax.axis_size(axis)
    return lax.ppermute(value, axis, [(i, (i + by) % count) for i in range(count)])


vmem = pl.BlockSpec(memory_space=pltpu.VMEM)
smem = pl.BlockSpec(memory_space=pltpu.SMEM)
hbm = pl.BlockSpec(memory_space=pltpu.HBM)


def held(value):
    return pltpu.with_memory_space_constraint(value, pltpu.HBM)


def room(mib):
    return pltpu.CompilerParams(vmem_limit_bytes=mib << 20)


def call_border(field):
    _, cx, cy, nz = field.shape
    return pl.pallas_call(
        border_kernel,
        name="border",
        in_specs=[hbm],
        out_specs=[vmem] * 4,
        scratch_shapes=[
            pltpu.VMEM((3, cx, 8, nz), f32),
            pltpu.VMEM((3, cx, 8, nz), f32),
            pltpu.SemaphoreType.DMA((4,)),
        ],
        out_shape=[
            jax.ShapeDtypeStruct((3, cy, nz), f32),
            jax.ShapeDtypeStruct((3, cy, nz), f32),
            jax.ShapeDtypeStruct((3, cx, nz), f32),
            jax.ShapeDtypeStruct((3, cx, nz), f32),
        ],
        compiler_params=room(8),
    )(held(field))


def call_sample(direction, halo, wind, wind_gradient, viscosity, cells, owner, gate, owners):
    _, cx, cy, nz = direction.shape
    tiles = cells.shape[0]
    return pl.pallas_call(
        sample_kernel,
        name="sample",
        in_specs=[hbm, vmem, vmem, vmem, vmem, hbm, hbm, hbm, vmem, vmem, vmem],
        out_specs=[vmem, vmem],
        scratch_shapes=[
            pltpu.VMEM((3, cx + 2, cy, nz), f32),
            pltpu.VMEM((3, cx, cy, nz), f32),
            pltpu.VMEM((9, cx, cy, nz), f32),
            pltpu.VMEM((cx, cy, nz), f32),
            pltpu.VMEM((3, cx * cy, 2 * nz), bf16),
            pltpu.VMEM((3, tiles, tile), f32),
            pltpu.VMEM((owners, lanes), f32),
            pltpu.VMEM((tile, tile), bf16),
            pltpu.VMEM((2 * owners, 2 * lanes), f32),
            pltpu.SMEM((tiles, tile), i32),
            pltpu.SemaphoreType.DMA((4, cx)),
            pltpu.SemaphoreType.DMA,
        ],
        out_shape=[
            jax.ShapeDtypeStruct((2, owners // 2, 4, lanes), f32),
            jax.ShapeDtypeStruct((tiles, tile), i32),
        ],
        compiler_params=room(40),
    )(held(direction), *halo, held(wind), held(wind_gradient), held(viscosity), cells, owner, gate)


def call_owner(gate_counts, got, sight, precision):
    owners = got.shape[0]
    return pl.pallas_call(
        owner_kernel,
        name="owner",
        in_specs=[smem, vmem, vmem, vmem],
        out_specs=[vmem, vmem],
        scratch_shapes=[pltpu.VMEM((owners // 8, lanes, 8 * lanes), bf16)],
        out_shape=[
            jax.ShapeDtypeStruct((owners, 1, 3 * lanes), f32),
            jax.ShapeDtypeStruct((1, sight.shape[2]), f32),
        ],
        compiler_params=room(24),
    )(gate_counts, got, sight, precision)


def call_scatter(returned, cells, slot, wind, wind_gradient, viscosity):
    _, cx, cy, nz = wind.shape
    tiles = cells.shape[0]
    half = returned.shape[0] // 2
    return pl.pallas_call(
        scatter_kernel,
        name="scatter",
        in_specs=[vmem, vmem, vmem, hbm, hbm, hbm],
        out_specs=[vmem] * 8,
        scratch_shapes=[
            pltpu.VMEM((6 * half, 2 * lanes), bf16),
            pltpu.VMEM((3, tiles, tile), f32),
            pltpu.SMEM((tiles, tile), i32),
            pltpu.SemaphoreType.DMA((3,)),
            pltpu.SemaphoreType.DMA,
        ],
        out_shape=[
            jax.ShapeDtypeStruct((3, cx * cy, nz), f32),
            jax.ShapeDtypeStruct(wind.shape, f32),
            jax.ShapeDtypeStruct(wind_gradient.shape, f32),
            jax.ShapeDtypeStruct(viscosity.shape, f32),
            jax.ShapeDtypeStruct((3, cy, nz), f32),
            jax.ShapeDtypeStruct((3, cy, nz), f32),
            jax.ShapeDtypeStruct((3, cx, nz), f32),
            jax.ShapeDtypeStruct((3, cx, nz), f32),
        ],
        compiler_params=room(24),
    )(returned, cells, slot, held(wind), held(wind_gradient), held(viscosity))


def border_shapes(cx, cy, nz):
    return [(3, cy, nz), (3, cy, nz), (3, cx - 2, 8, nz), (3, cx - 2, 8, nz)]


def call_adjoint(pulled, wind, wind_gradient, viscosity):
    _, cx, cy, nz = wind.shape
    shapes = [(3, cx, cy, nz)] + border_shapes(cx, cy, nz)
    return pl.pallas_call(
        adjoint_kernel,
        name="adjoint",
        in_specs=[vmem] * 4,
        out_specs=[hbm] + [vmem] * 4,
        scratch_shapes=[pltpu.VMEM((3, cx + 2, cy, nz), f32), pltpu.SemaphoreType.DMA((cx,))],
        out_shape=[jax.ShapeDtypeStruct(shape, f32) for shape in shapes],
        compiler_params=room(24),
    )(pulled, wind, wind_gradient, viscosity)


def call_edges(result, sides, halo):
    _, cx, cy, nz = result.shape
    return pl.pallas_call(
        edge_kernel,
        name="edges",
        in_specs=[hbm] + [vmem] * 8,
        out_specs=hbm,
        scratch_shapes=[pltpu.VMEM(shape, f32) for shape in border_shapes(cx, cy, nz)]
        + [pltpu.SemaphoreType.DMA((4,))],
        out_shape=jax.ShapeDtypeStruct(result.shape, f32),
        input_output_aliases={0: 0},
        compiler_params=room(16),
    )(result, *sides, *halo)


def body(
    direction,
    wind,
    wind_gradient,
    viscosity,
    sample_owner,
    sample_cell,
    sample_gate,
    sight,
    gate_counts,
    precision,
):
    owners = lax.axis_size("track") * lax.axis_size("cross")
    names = ("track", "cross")
    xlo, xhi, ylo, yhi = call_border(direction)
    halo = (
        shifted(xhi, "track", 1),
        shifted(xlo, "track", -1),
        shifted(yhi, "cross", 1),
        shifted(ylo, "cross", -1),
    )
    cells, owner, gate = [
        v.reshape(-1, tile)
        for v in lax.sort(
            (sample_cell.reshape(-1), sample_owner.reshape(-1), sample_gate.reshape(-1)), num_keys=1, is_stable=False
        )
    ]
    slots, slot = call_sample(direction, halo, wind, wind_gradient, viscosity, cells, owner, gate, owners)
    got = lax.all_to_all(slots.reshape(owners, 4, lanes), names, split_axis=0, concat_axis=0, tiled=True)
    back, weighted = call_owner(gate_counts, got, sight, precision)
    returned = lax.all_to_all(back, names, split_axis=0, concat_axis=0, tiled=True)
    *taken, xlo, xhi, ylo, yhi = call_scatter(returned, cells, slot, wind, wind_gradient, viscosity)
    halo = (
        shifted(xhi, "track", 1),
        shifted(xlo, "track", -1),
        shifted(yhi, "cross", 1),
        shifted(ylo, "cross", -1),
    )
    result, *sides = call_adjoint(*taken)
    result = call_edges(result, sides, halo)
    return (result, weighted)


def solution(mesh):
    placed = (
        P(None, "track", "cross", None),
        P(None, "track", "cross", None),
        P(None, "track", "cross", None),
        P("track", "cross", None),
        P("track", "cross", None, None),
        P("track", "cross", None),
        P("track", "cross", None),
        P(None, ("track", "cross"), None),
        P(("track", "cross"), None),
        P(("track", "cross"), None, None),
    )
    return jax.shard_map(
        body,
        mesh=mesh,
        in_specs=placed,
        out_specs=(P(None, "track", "cross", None), P(("track", "cross"), None)),
        check_vma=False,
    )
```
